32 devices in a mesh: seq: 8 (over y, x, core), pipe: 4 (over z).
Axes of the slice: x: 2, y: 2, z: 4, core: 2. Of those that a mesh axis runs over, the one named last changes fastest.
Arguments:
- query_in: bfloat16 [4, 1024, 4096], P('pipe', 'seq'), may hold values from -6 to 6
- key_in: bfloat16 [4, 1024, 4096], P('pipe', 'seq'), may hold values from -6 to 6
- value_in: bfloat16 [4, 1024, 4096], P('pipe', 'seq'), may hold values from -6 to 6
- grad_out: bfloat16 [4, 1024, 4096], P('pipe', 'seq'), may hold values from -6 to 6
- long_filter: float32 [4, 1024, 256], P('pipe', 'seq'), may hold values from -2 to 2, as said below
- short_taps: float32 [4, 3, 3, 4096], P('pipe'), may hold values from -3 to 3
Outputs:
- layer_out: bfloat16 [4, 1024, 4096], P('pipe', 'seq')
- passed_grads: bfloat16 [4, 3, 1024, 4096], P('pipe', None, 'seq')
- filter_grad: float32 [4, 1024, 256], P('pipe', 'seq')
- tap_grads: float32 [4, 3, 3, 4096], P('pipe')
The draws below stay inside these ranges and needn't reach their ends.
Inputs may be any that keep to these rules, and one draw needn't show every extreme that they name: `long_filter`: one filter for each channel group of each section.
All inputs are finite; a program needn't handle non-finite values.
Results may differ from the reference program's by a relative error of at most 0.005.
Values may be sent and summed in bfloat16 or wider, within the bound.
No kernel may reach another device: no remote copies, remote signals or barrier semaphores. Data moves between devices by JAX's collectives and lax.ppermute only.
A program may use at most 256 MiB of HBM per device.

```python
import math
import jax
import jax.numpy as jnp
from jax import lax

GW = 16
GROUP_COUNT = 256
D = 4096
TAPS = 3
TOKEN_LENGTH = 1024
SECTION_COUNT = 4


def draw_long_filter(key, part):
    split_random_keys = jax.random.split(key, 7)
    slow_count = 5
    random_noise = jnp.clip(jax.random.normal(split_random_keys[0], (SECTION_COUNT, TOKEN_LENGTH, GROUP_COUNT)), -4.0, 4.0)
    is_slow = jax.random.randint(split_random_keys[1], (SECTION_COUNT, 1, GROUP_COUNT), 0, 10) < slow_count
    slow_rate = jnp.exp(jax.random.uniform(split_random_keys[2], (SECTION_COUNT, 1, GROUP_COUNT), minval=math.log(0.25), maxval=math.log(0.5))) / TOKEN_LENGTH
    fast_rate = jnp.exp(jax.random.uniform(split_random_keys[3], (SECTION_COUNT, 1, GROUP_COUNT), minval=math.log(0.02), maxval=math.log(0.05)))
    spike_position = jax.random.randint(split_random_keys[4], (SECTION_COUNT, 1, GROUP_COUNT, 2), 1, TOKEN_LENGTH)
    spike_height = jax.random.uniform(split_random_keys[5], (SECTION_COUNT, 1, GROUP_COUNT, 2), minval=0.22, maxval=0.69)
    tail_share = jax.random.uniform(split_random_keys[6], (SECTION_COUNT, 1, GROUP_COUNT), minval=0.2, maxval=0.3)
    token_place = jnp.arange(TOKEN_LENGTH, dtype=jnp.int32)
    reached_mask = (token_place[None, :, None, None] >= spike_position).astype(jnp.float32)
    spike_total = jnp.sum(reached_mask * spike_height, axis=3)
    step_values_real = token_place.astype(jnp.float32)[None, :, None]
    slow_amplitude = jnp.sqrt(1.0 - jnp.exp(-2.0 * slow_rate))
    fast_amplitude = jnp.sqrt(1.0 - jnp.exp(-2.0 * fast_rate))
    lasting = jnp.exp(-slow_rate * step_values_real - spike_total)
    fading = jnp.exp(-fast_rate * step_values_real)
    envelope = jnp.where(is_slow, slow_amplitude * lasting, fast_amplitude * (fading + tail_share * lasting))
    return random_noise * envelope


def levels(own_key, dims, shards, least, largest):
    factor_of = 1.0
    for dim, blocks in shards:
        draws = jax.random.uniform(jax.random.fold_in(jax.random.fold_in(own_key, 6), dim), (blocks,), jnp.float32, least / len(shards), largest / len(shards))
        factor_of = factor_of * jnp.repeat(jnp.exp(draws), dims[dim] // blocks).reshape((-1,) + (1,) * (len(dims) - 1 - dim))
    return factor_of


def bell_draw(key, dims, spread, limit, pieces=(), kind=jnp.bfloat16):
    loudness = levels(key, dims, pieces, -0.22, 0.18) if pieces else 1.0
    drawn = jax.random.normal(key, dims, jnp.float32) * spread * loudness
    return jnp.minimum(jnp.maximum(drawn, -limit), limit).astype(kind)


def setup_inputs(seed: int = 0) -> dict:
    arg_keys = jax.random.split(jax.random.key(seed), 7)
    return {
        "query_in": bell_draw(arg_keys[0], (SECTION_COUNT, TOKEN_LENGTH, D), 1.0, 6.0, ((0, 4), (1, 8))),
        "key_in": bell_draw(arg_keys[1], (SECTION_COUNT, TOKEN_LENGTH, D), 1.0, 6.0, ((0, 4), (1, 8))),
        "value_in": bell_draw(arg_keys[2], (SECTION_COUNT, TOKEN_LENGTH, D), 1.0, 6.0, ((0, 4), (1, 8))),
        "grad_out": bell_draw(arg_keys[3], (SECTION_COUNT, TOKEN_LENGTH, D), 1.0, 6.0, ((0, 4), (1, 8))),
        "long_filter": draw_long_filter(jax.random.fold_in(arg_keys[6], 71), 0),
        "short_taps": bell_draw(arg_keys[5], (SECTION_COUNT, 3, TAPS, D), 0.6, 3.0, ((0, 4),), jnp.float32),
    }


def short_filter(tap_table, padded, length):
    result = tap_table[:, 0, None, :] * padded[:, 2:2 + length, :]
    result = result + tap_table[:, 1, None, :] * padded[:, 1:1 + length, :]
    result = result + tap_table[:, 2, None, :] * padded[:, 0:length, :]
    return result

def one_section(inputs):
    query_in, key_in, value_in, grad_out, long_filter, short_taps = inputs
    length = query_in.shape[0]
    fft_size = 2 * length
    stacked_in = jnp.stack([query_in, key_in, value_in]).astype(jnp.float32)
    padded = jnp.pad(stacked_in, ((0, 0), (2, 0), (0, 0)))
    featured = short_filter(short_taps, padded, length)
    query_feat = featured[0]
    keyed = featured[1]
    valued = featured[2]
    grad_float = grad_out.astype(jnp.float32)
    product = (keyed * valued).astype(jnp.bfloat16)
    scaled = (grad_float * query_feat).astype(jnp.bfloat16)
    filter_spec = jnp.fft.rfft(long_filter, n=fft_size, axis=0)
    kernel = jnp.repeat(filter_spec, GW, axis=1)
    prod_spec = jnp.fft.rfft(product.astype(jnp.float32), n=fft_size, axis=0)
    conv_out = jnp.fft.irfft(prod_spec * kernel, n=fft_size, axis=0)[:length]
    layer_out = (query_feat * conv_out).astype(jnp.bfloat16)
    scaled_spec = jnp.fft.rfft(scaled.astype(jnp.float32), n=fft_size, axis=0)
    back_out = jnp.fft.irfft(scaled_spec * jnp.conj(kernel), n=fft_size, axis=0)[:length]
    cross_spec = (scaled_spec * jnp.conj(prod_spec)).reshape(-1, GROUP_COUNT, GW).sum(axis=2)
    filter_grad = jnp.fft.irfft(cross_spec, n=fft_size, axis=0)[:length] / math.sqrt(length * GW)
    grad_stack = jnp.stack([grad_float * conv_out, back_out * valued, back_out * keyed])
    after_rows = jnp.pad(grad_stack, ((0, 0), (0, 2), (0, 0)))
    input_grads = short_taps[:, 0, None, :] * after_rows[:, 0:length, :]
    input_grads = input_grads + short_taps[:, 1, None, :] * after_rows[:, 1:1 + length, :]
    input_grads = input_grads + short_taps[:, 2, None, :] * after_rows[:, 2:2 + length, :]
    input_grads = input_grads.astype(jnp.bfloat16)
    tap_grads = jnp.stack([lax.optimization_barrier(jnp.sum(grad_stack * padded[:, 2 - tap_lag:2 - tap_lag + length, :], axis=1)) for tap_lag in range(3)], axis=1) / math.sqrt(length)
    return (layer_out, input_grads, filter_grad, tap_grads)

def reference(query_in, key_in, value_in, grad_out, long_filter, short_taps):
    layer_out, input_grads, filter_grad, tap_grads = lax.map(one_section, (query_in, key_in, value_in, grad_out, long_filter, short_taps))
    passed_grads = jnp.concatenate([input_grads[1:], jnp.zeros_like(input_grads[:1])], axis=0)
    return (layer_out, passed_grads, filter_grad, tap_grads)
```

```python
import functools
import math

import jax
import jax.numpy as jnp
from jax import lax
from jax.experimental import pallas as pl
from jax.experimental.pallas import tpu as pltpu
from jax.sharding import PartitionSpec as P

F32 = jnp.float32
BF16 = jnp.bfloat16
CHUNKS = 1
TILE = 16
LANES = 128


def passed_along(x, axis, by):
    count = lax.axis_size(axis)
    pairs = [(i, i + by) for i in range(count) if 0 <= i + by < count]
    return lax.ppermute(x, axis, pairs)


def exchange(x):
    return lax.all_to_all(x, "seq", split_axis=0, concat_axis=0, tiled=True)


def dot_nt(left, right):
    return lax.dot_general(
        left, right, (((1,), (1,)), ((), ())), preferred_element_type=F32
    )


def dot_nn(left, right):
    return lax.dot_general(
        left, right, (((1,), (0,)), ((), ())), preferred_element_type=F32
    )


def grid_index(shape, dim):
    return lax.broadcasted_iota(jnp.int32, shape, dim)


def identity(size):
    shape = (size, size)
    return (grid_index(shape, 0) == grid_index(shape, 1)).astype(F32).astype(BF16)


def delayed(x, before):
    row = grid_index(x.shape, 0)
    one = jnp.where(row == 0, before[1:2], pltpu.roll(x, 1, 0))
    two = jnp.where(row == 0, before[0:1], pltpu.roll(x, 2, 0))
    two = jnp.where(row == 1, before[1:2], two)
    return one, two


def advanced(x, after):
    rows = x.shape[0]
    row = grid_index(x.shape, 0)
    one = jnp.where(row == rows - 1, after[0:1], pltpu.roll(x, rows - 1, 0))
    two = jnp.where(row == rows - 1, after[1:2], pltpu.roll(x, rows - 2, 0))
    two = jnp.where(row == rows - 2, after[0:1], two)
    return one, two


def featured_of(taps, branch, x, one, two):
    base = 3 * branch
    out = taps[base : base + 1] * x
    out = out + taps[base + 1 : base + 2] * one
    return out + taps[base + 2 : base + 3] * two


def send_kernel(query_ref, key_ref, value_ref, grad_ref, before_ref, taps_ref, filter_ref, out_ref):
    own = query_ref.shape[1]
    groups = filter_ref.shape[0]
    unit = identity(LANES)
    for lane in range(0, own, LANES):
        cols = pl.ds(lane, LANES)
        taps = taps_ref[:, cols]
        feats = []
        for branch, ref in enumerate((query_ref, key_ref, value_ref)):
            x = ref[:, cols].astype(F32)
            one, two = delayed(x, before_ref[branch, :, cols].astype(F32))
            feats.append(featured_of(taps, branch, x, one, two))
        product = (feats[1] * feats[2]).astype(BF16)
        scaled = (grad_ref[:, cols].astype(F32) * feats[0]).astype(BF16)
        out_ref[0, pl.ds(lane, LANES), :] = dot_nt(unit, product).astype(BF16)
        out_ref[0, pl.ds(own + lane, LANES), :] = dot_nt(unit, scaled).astype(BF16)
    tail = out_ref.shape[1] - 2 * own
    taken = filter_ref[...]
    if tail > groups:
        taken = jnp.concatenate([taken, jnp.zeros((tail - groups, LANES), F32)], axis=0)
    out_ref[0, pl.ds(2 * own, tail), :] = taken.astype(BF16)


def conv_kernel(own, groups, scale, in_ref, out_ref, corr_ref, first_pad, second_pad, taps):
    blocks = in_ref.shape[0]
    wide = own // groups
    rows = blocks * wide
    skip = rows - wide
    lane = grid_index((LANES, LANES), 1)
    sub = grid_index((LANES, LANES), 0)
    flip = (lane + sub == LANES - 1).astype(F32).astype(BF16)
    first_pad[pl.ds(0, skip), :] = jnp.zeros((skip, LANES), BF16)
    second_pad[pl.ds(rows, skip), :] = jnp.zeros((skip, LANES), BF16)
    held = in_ref[:, pl.ds(2 * own, in_ref.shape[1] - 2 * own), :].astype(F32)
    taps[...] = held

    def one_group(g, carry):
        at = pl.multiple_of(g * wide, wide)
        first = in_ref[:, pl.ds(at, wide), :].reshape(rows, LANES)
        second = in_ref[:, pl.ds(own + at, wide), :].reshape(rows, LANES)
        first_pad[pl.ds(skip, rows), :] = first
        second_pad[pl.ds(0, rows), :] = second
        turned = []
        for k in range(blocks):
            line = taps[k, pl.ds(g, 1), :]
            spread = jnp.broadcast_to(line, (LANES, LANES))
            turned.append(pltpu.roll(spread, 0, 1, stride=1, stride_axis=0))
        toeplitz = []
        for k in range(blocks):
            lower = turned[k - 1] if k else jnp.zeros((LANES, LANES), F32)
            toeplitz.append(jnp.where(lane >= sub, turned[k], lower).astype(BF16))
        shifted = [first_pad[pl.ds(skip - wide * k, rows), :] for k in range(blocks)]
        ahead = [second_pad[pl.ds(wide * k, rows), :] for k in range(blocks)]
        ahead = jnp.concatenate(ahead, axis=1)
        conv = dot_nn(jnp.concatenate(shifted, axis=1), jnp.concatenate(toeplitz, axis=0))
        back = dot_nt(ahead, jnp.concatenate(toeplitz, axis=1))
        out_ref[:, pl.ds(at, wide), :] = conv.astype(BF16).reshape(blocks, wide, LANES)
        out_ref[:, pl.ds(own + at, wide), :] = back.astype(BF16).reshape(blocks, wide, LANES)
        backwards = dot_nt(flip, first).astype(BF16)
        cross = dot_nn(backwards, ahead)
        rolled = [
            pltpu.roll(cross[:, k * LANES : (k + 1) * LANES], 1, 1, stride=1, stride_axis=0)
            for k in range(blocks)
        ]
        for k in range(blocks):
            later = rolled[k + 1] if k + 1 < blocks else jnp.zeros((LANES, LANES), F32)
            mixed = jnp.where(lane <= sub, rolled[k], later)
            corr_ref[k, pl.ds(g, 1), :] = jnp.sum(mixed, axis=0, keepdims=True) * scale
        return carry

    lax.fori_loop(0, groups, one_group, 0)
    pick_row = grid_index((TILE, 2 * LANES), 0)
    pick_lane = grid_index((TILE, 2 * LANES), 1)
    for a in range(blocks):
        total = jnp.zeros((TILE, LANES), F32)
        if a + 1 < blocks:
            for part in range(own // LANES):
                local_row = pick_row - 4 * part
                wanted = (local_row // 2) * LANES + local_row % 2
                used = (local_row >= 0) & (local_row < 4) & (pick_lane == wanted)
                both = jnp.concatenate(
                    [
                        out_ref[a + 1, pl.ds(part * LANES, LANES), :],
                        out_ref[a + 1, pl.ds(own + part * LANES, LANES), :],
                    ],
                    axis=1,
                )
                total = total + dot_nt(used.astype(F32).astype(BF16), both)
        out_ref[a, pl.ds(2 * own, TILE), :] = total.astype(BF16)


def finish_kernel(
    scale, has_old, query_ref, key_ref, value_ref, grad_ref, before_ref, after_ref, taps_ref, in_ref, *refs
):
    layer_ref, grads_ref, sums_ref = refs[1:] if has_old else refs
    own = query_ref.shape[1]
    rows = query_ref.shape[0]
    unit = identity(LANES)
    for part in range(own // LANES):
        cols = pl.ds(part * LANES, LANES)
        taps = taps_ref[:, cols]
        conv = dot_nt(unit, in_ref[0, pl.ds(part * LANES, LANES), :])
        back = dot_nt(unit, in_ref[0, pl.ds(own + part * LANES, LANES), :])
        edge = in_ref[0, pl.ds(2 * own, TILE), :].astype(F32)[4 * part : 4 * part + 4]
        raw = []
        feats = []
        nexts = []
        for branch, ref in enumerate((query_ref, key_ref, value_ref)):
            x = ref[:, cols].astype(F32)
            one, two = delayed(x, before_ref[branch, :, cols].astype(F32))
            raw.append((x, one, two))
            feats.append(featured_of(taps, branch, x, one, two))
            if branch:
                new = after_ref[branch - 1, :, cols].astype(F32)
                last = x[rows - 2 : rows]
                new_one = jnp.concatenate([last[1:2], new[0:1]], axis=0)
                nexts.append(featured_of(taps, branch, new, new_one, last))
        grad = grad_ref[:, cols].astype(F32)
        grad_next = after_ref[2, :, cols].astype(F32)
        layer_ref[:, cols] = (feats[0] * conv).astype(BF16)
        grads = (grad * conv, back * feats[2], back * feats[1])
        follow = (grad_next * edge[0:2], edge[2:4] * nexts[1], edge[2:4] * nexts[0])
        lines = []
        for branch in range(3):
            value = grads[branch]
            one, two = advanced(value, follow[branch])
            base = 3 * branch
            total = taps[base : base + 1] * value
            total = total + taps[base + 1 : base + 2] * one
            total = total + taps[base + 2 : base + 3] * two
            grads_ref[branch, :, cols] = total.astype(BF16)
            for lag in range(3):
                lines.append(jnp.sum(value * raw[branch][lag], axis=0, keepdims=True) * scale)
        lines.append(jnp.zeros((TILE - 9, LANES), F32))
        sums_ref[0, :, cols] = jnp.concatenate(lines, axis=0)


def local(query_in, key_in, value_in, grad_out, long_filter, short_taps):
    seq = lax.axis_size("seq")
    rows, width = query_in.shape[1:]
    groups = long_filter.shape[2]
    total_rows = rows * seq
    wide = width // groups
    chunks = min(CHUNKS, width // (LANES * seq))
    own = width // (chunks * seq)
    own_groups = own // wide
    tail = -(-own_groups // TILE) * TILE
    query, key, value, grad = query_in[0], key_in[0], value_in[0], grad_out[0]
    taps = short_taps[0].reshape(9, width)
    last = jnp.stack([query[rows - 2 :], key[rows - 2 :], value[rows - 2 :]])
    before = passed_along(last, "seq", 1)
    top = jnp.stack([key[:2], value[:2], grad[:2]])
    after = passed_along(top, "seq", -1)
    filter_t = long_filter[0].T

    layer = None
    corr_parts, sum_parts, grad_parts = [], [], []
    for chunk in range(chunks):
        base = chunk * seq
        main = pl.BlockSpec((rows, own), lambda d, base=base: (0, base + d))
        edge = pl.BlockSpec((3, 2, own), lambda d, base=base: (0, 0, base + d))
        tap_spec = pl.BlockSpec((9, own), lambda d, base=base: (0, base + d))
        sent = pl.pallas_call(
            send_kernel,
            grid=(seq,),
            in_specs=[
                main, main, main, main, edge, tap_spec,
                pl.BlockSpec((own_groups, rows), lambda d, base=base: (base + d, 0)),
            ],
            out_specs=pl.BlockSpec((1, 2 * own + tail, rows), lambda d: (d, 0, 0)),
            out_shape=jax.ShapeDtypeStruct((seq, 2 * own + tail, rows), BF16),
            name="send",
        )(query, key, value, grad, before, taps, filter_t)
        arrived = exchange(sent)
        returned, corr = pl.pallas_call(
            functools.partial(conv_kernel, own, own_groups, 1.0 / math.sqrt(total_rows * wide)),
            in_specs=[pl.BlockSpec(memory_space=pltpu.VMEM)],
            out_specs=[pl.BlockSpec(memory_space=pltpu.VMEM)] * 2,
            out_shape=[
                jax.ShapeDtypeStruct((seq, 2 * own + TILE, rows), BF16),
                jax.ShapeDtypeStruct((seq, own_groups, rows), F32),
            ],
            scratch_shapes=[
                pltpu.VMEM((2 * seq * wide - wide, LANES), BF16),
                pltpu.VMEM((2 * seq * wide - wide, LANES), BF16),
                pltpu.VMEM((seq, tail, LANES), F32),
            ],
            name="conv",
        )(arrived)
        back = exchange(returned)
        corr_parts.append(corr)
        has_old = layer is not None
        extra = (layer,) if has_old else ()
        layer, grads, sums = pl.pallas_call(
            functools.partial(finish_kernel, 1.0 / math.sqrt(total_rows), has_old),
            grid=(seq,),
            in_specs=[
                main, main, main, main, edge, edge, tap_spec,
                pl.BlockSpec((1, 2 * own + TILE, rows), lambda d: (d, 0, 0)),
            ] + [pl.BlockSpec(memory_space=pl.ANY)] * len(extra),
            out_specs=[
                main,
                pl.BlockSpec((3, rows, own), lambda d: (0, 0, d)),
                pl.BlockSpec((1, TILE, own), lambda d: (d, 0, 0)),
            ],
            out_shape=[
                jax.ShapeDtypeStruct((rows, width), BF16),
                jax.ShapeDtypeStruct((3, rows, own * seq), BF16),
                jax.ShapeDtypeStruct((seq, TILE, own), F32),
            ],
            input_output_aliases={8: 0} if has_old else {},
            name="finish",
        )(query, key, value, grad, before, after, taps, back, *extra)
        grad_parts.append(passed_along(grads, "pipe", -1))
        sum_parts.append(sums)

    corr = exchange(jnp.stack(corr_parts, axis=1))
    filter_grad = jnp.transpose(corr, (3, 1, 0, 2)).reshape(rows, groups)
    sums = jnp.sum(exchange(jnp.stack(sum_parts, axis=1)), axis=0)
    sums = exchange(jnp.broadcast_to(sums[None], (seq,) + sums.shape))
    tap_grads = jnp.transpose(sums[:, :, :9], (2, 1, 0, 3)).reshape(3, 3, width)
    passed_grads = jnp.concatenate(grad_parts, axis=2)
    return (layer[None], passed_grads[None], filter_grad[None], tap_grads[None])


def solution(mesh):
    in_specs = (
        P("pipe", "seq", None),
        P("pipe", "seq", None),
        P("pipe", "seq", None),
        P("pipe", "seq", None),
        P("pipe", "seq", None),
        P("pipe", None, None, None),
    )
    out_specs = (
        P("pipe", "seq", None),
        P("pipe", None, "seq", None),
        P("pipe", "seq", None),
        P("pipe", None, None, None),
    )
    return jax.shard_map(local, mesh=mesh, in_specs=in_specs, out_specs=out_specs, check_vma=False)
```

```python
import functools
import math

import jax
import jax.numpy as jnp
from jax import lax
from jax.experimental import pallas as pl
from jax.experimental.pallas import tpu as pltpu
from jax.sharding import PartitionSpec as P


F32 = jnp.float32
BF16 = jnp.bfloat16
GROUPS_AT_ONCE = 2
SPAN = 4
TILE = 16
LANES = 128


def passed_along(x, axis, by):
    count = lax.axis_size(axis)
    pairs = [(i, i + by) for i in range(count) if 0 <= i + by < count]
    return lax.ppermute(x, axis, pairs)


def exchange(x):
    return lax.all_to_all(x, "seq", split_axis=0, concat_axis=0, tiled=True)


def dot_nt(left, right):
    return lax.dot_general(
        left, right, (((1,), (1,)), ((), ())), preferred_element_type=F32
    )


def dot_nn(left, right):
    return lax.dot_general(
        left, right, (((1,), (0,)), ((), ())), preferred_element_type=F32
    )


def grid_index(shape, dim):
    return lax.broadcasted_iota(jnp.int32, shape, dim)


def identity(size):
    shape = (size, size)
    return (grid_index(shape, 0) == grid_index(shape, 1)).astype(F32).astype(BF16)


def patched_head(x, first_rows):
    return jnp.concatenate([first_rows, x[8:]], axis=0)


def patched_tail(x, last_rows):
    return jnp.concatenate([x[:-8], last_rows], axis=0)


def delayed(x, before):
    row = grid_index((8, x.shape[1]), 0)
    one = pltpu.roll(x, 1, 0)
    one = patched_head(one, jnp.where(row == 0, before[1:2], one[:8]))
    two = pltpu.roll(x, 2, 0)
    top = jnp.where(row == 0, before[0:1], jnp.where(row == 1, before[1:2], two[:8]))
    return one, patched_head(two, top)


def advanced(x, after):
    rows = x.shape[0]
    row = grid_index((8, x.shape[1]), 0)
    one = pltpu.roll(x, rows - 1, 0)
    one = patched_tail(one, jnp.where(row == 7, after[0:1], one[-8:]))
    two = pltpu.roll(x, rows - 2, 0)
    low = jnp.where(row == 7, after[1:2], jnp.where(row == 6, after[0:1], two[-8:]))
    return one, patched_tail(two, low)


def weighted(taps, branch, x, one, two):
    base = 3 * branch
    out = taps[base : base + 1] * x
    out = out + taps[base + 1 : base + 2] * one
    return out + taps[base + 2 : base + 3] * two


def next_featured(taps, branch, x, new):
    last = x[-8:][6:8]
    one = jnp.concatenate([last[1:2], new[0:1]], axis=0)
    return weighted(taps, branch, new, one, last)


def send_kernel(query_ref, key_ref, value_ref, grad_ref, before_ref, taps_ref, filter_ref, out_ref):
    seq, rows_out, _ = out_ref.shape
    groups = filter_ref.shape[0] // seq
    unit = identity(LANES)
    for d in range(seq):
        cols = pl.ds(d * LANES, LANES)
        taps = taps_ref[:, cols]
        feats = []
        for branch, ref in enumerate((query_ref, key_ref, value_ref)):
            x = ref[:, cols].astype(F32)
            one, two = delayed(x, before_ref[branch, :, cols].astype(F32))
            feats.append(weighted(taps, branch, x, one, two))
        product = (feats[1] * feats[2]).astype(BF16)
        scaled = (grad_ref[:, cols].astype(F32) * feats[0]).astype(BF16)
        out_ref[d, pl.ds(0, LANES), :] = dot_nt(unit, product).astype(BF16)
        out_ref[d, pl.ds(LANES, LANES), :] = dot_nt(unit, scaled).astype(BF16)
        taken = filter_ref[pl.ds(d * groups, groups), :]
        pad = jnp.zeros((rows_out - 2 * LANES - groups, LANES), F32)
        taken = jnp.concatenate([taken, pad], axis=0)
        out_ref[d, pl.ds(2 * LANES, rows_out - 2 * LANES), :] = taken.astype(BF16)


def toeplitz_blocks(lines):
    base = [
        pltpu.roll(jnp.broadcast_to(line, (8, LANES)), 0, 1, stride=1, stride_axis=0)
        for line in lines
    ]
    lane = grid_index((8, LANES), 1)
    sub = grid_index((8, LANES), 0)
    zero = jnp.zeros((8, LANES), F32)
    parts = [[] for _ in lines]
    for m in range(LANES // 8):
        below = zero
        for k, start in enumerate(base):
            turned = pltpu.roll(start, 8 * m, 1) if m else start
            parts[k].append(jnp.where(lane >= sub + 8 * m, turned, below))
            below = turned
    return [jnp.concatenate(part, axis=0).astype(BF16) for part in parts]


def diagonal_sums(cross, blocks):
    parts = [cross[:, k * LANES : (k + 1) * LANES] for k in range(blocks)]
    rows = LANES
    while rows > 8:
        half = rows // 2
        lane = grid_index((half, LANES), 1)
        turned = [pltpu.roll(part[half:rows], LANES - half, 1) for part in parts]
        turned.append(jnp.zeros((half, LANES), F32))
        parts = [
            parts[k][:half] + jnp.where(lane < LANES - half, turned[k], turned[k + 1])
            for k in range(blocks)
        ]
        rows = half
    lane = grid_index((8, LANES), 1)
    sub = grid_index((8, LANES), 0)
    turned = [pltpu.roll(part, LANES - 7, 1, stride=1, stride_axis=0) for part in parts]
    turned.append(jnp.zeros((8, LANES), F32))
    keep = lane < sub + (LANES - 7)
    return [
        jnp.sum(jnp.where(keep, turned[k], turned[k + 1]), axis=0, keepdims=True)
        for k in range(blocks)
    ]


def conv_kernel(groups, scale, in_ref, out_ref, corr_ref, taps):
    blocks = in_ref.shape[0]
    wide = LANES // groups
    rows = blocks * wide
    lane = grid_index((LANES, LANES), 1)
    sub = grid_index((LANES, LANES), 0)
    flipped = (sub // 8) * 8 + 7 - sub % 8
    flip = (lane == flipped).astype(F32).astype(BF16)
    taps[...] = in_ref[:, pl.ds(2 * LANES, in_ref.shape[1] - 2 * LANES), :].astype(F32)

    def one_group(g):
        at = pl.multiple_of(g * wide, wide)
        first = in_ref[:, pl.ds(at, wide), :].reshape(rows, LANES)
        second = in_ref[:, pl.ds(LANES + at, wide), :].reshape(rows, LANES)
        toeplitz = toeplitz_blocks([taps[k, pl.ds(g, 1), :] for k in range(blocks)])
        shifted, ahead = [first], [second]
        for k in range(1, blocks):
            gap = jnp.zeros((wide * k, LANES), BF16)
            shifted.append(jnp.concatenate([gap, first[: rows - wide * k]], axis=0))
            ahead.append(jnp.concatenate([second[wide * k :], gap], axis=0))
        ahead = jnp.concatenate(ahead, axis=1)
        conv = dot_nn(jnp.concatenate(shifted, axis=1), jnp.concatenate(toeplitz, axis=0))
        back = dot_nt(ahead, jnp.concatenate(toeplitz, axis=1))
        out_ref[:, pl.ds(at, wide), :] = conv.astype(BF16).reshape(blocks, wide, LANES)
        out_ref[:, pl.ds(LANES + at, wide), :] = back.astype(BF16).reshape(blocks, wide, LANES)
        cross = dot_nn(dot_nt(flip, first).astype(BF16), ahead)
        for k, line in enumerate(diagonal_sums(cross, blocks)):
            corr_ref[k, pl.ds(g, 1), :] = line * scale

    together = GROUPS_AT_ONCE if groups % GROUPS_AT_ONCE == 0 else 1

    def some_groups(step, carry):
        for part in range(together):
            one_group(step * together + part)
        return carry

    lax.fori_loop(0, groups // together, some_groups, 0)
    pick_row = grid_index((TILE, 2 * LANES), 0)
    pick_lane = grid_index((TILE, 2 * LANES), 1)
    wanted = (pick_row // 2) * LANES + pick_row % 2
    pick = ((pick_row < 4) & (pick_lane == wanted)).astype(F32).astype(BF16)
    for a in range(blocks):
        if a + 1 < blocks:
            both = [out_ref[a + 1, pl.ds(0, LANES), :], out_ref[a + 1, pl.ds(LANES, LANES), :]]
            line = dot_nt(pick, jnp.concatenate(both, axis=1)).astype(BF16)
        else:
            line = jnp.zeros((TILE, LANES), BF16)
        out_ref[a, pl.ds(2 * LANES, TILE), :] = line


def finish_kernel(
    scale, has_old, query_ref, key_ref, value_ref, grad_ref, before_ref, after_ref, taps_ref, in_ref, *refs
):
    layer_ref, late_ref, sums_ref = refs[1:] if has_old else refs
    rows = query_ref.shape[0]
    unit = identity(LANES)
    for part in range(in_ref.shape[0]):
        cols = pl.ds(part * LANES, LANES)
        taps = taps_ref[:, cols]
        conv = dot_nt(unit, in_ref[part, pl.ds(0, LANES), :])
        back = dot_nt(unit, in_ref[part, pl.ds(LANES, LANES), :])
        edge = in_ref[part, pl.ds(2 * LANES, TILE), :].astype(F32)
        grad = grad_ref[:, cols].astype(F32)
        lines = []

        def tap_lines(value, raw):
            for shifted in raw:
                lines.append(jnp.sum(value * shifted, axis=0, keepdims=True) * scale)

        x = query_ref[:, cols].astype(F32)
        raw = (x,) + delayed(x, before_ref[0, :, cols].astype(F32))
        layer_ref[:, cols] = (weighted(taps, 0, *raw) * conv).astype(BF16)
        value = grad * conv
        tap_lines(value, raw)
        follow = after_ref[2, :, cols].astype(F32) * edge[0:2]
        late_ref[pl.ds(0, rows), cols] = weighted(taps, 0, value, *advanced(value, follow)).astype(BF16)
        x = key_ref[:, cols].astype(F32)
        key_raw = (x,) + delayed(x, before_ref[1, :, cols].astype(F32))
        x = value_ref[:, cols].astype(F32)
        value_raw = (x,) + delayed(x, before_ref[2, :, cols].astype(F32))
        tap_lines(back * weighted(taps, 2, *value_raw), key_raw)
        tap_lines(back * weighted(taps, 1, *key_raw), value_raw)
        late_ref[pl.ds(rows, rows), cols] = back.astype(BF16)
        tail = jnp.concatenate([edge[2:4], jnp.zeros((TILE - 2, LANES), F32)], axis=0)
        late_ref[pl.ds(2 * rows, TILE), cols] = tail.astype(BF16)
        lines.append(jnp.zeros((TILE - 9, LANES), F32))
        sums_ref[:, cols] = jnp.concatenate(lines, axis=0)


def apply_kernel(has_old, key_ref, value_ref, before_ref, after_ref, taps_ref, late_ref, *refs):
    out_ref = refs[1] if has_old else refs[0]
    rows, width = key_ref.shape
    for part in range(width // LANES):
        cols = pl.ds(part * LANES, LANES)
        taps = taps_ref[:, cols]
        back = late_ref[pl.ds(rows, rows), cols].astype(F32)
        edge = late_ref[pl.ds(2 * rows, TILE), cols].astype(F32)[0:2]
        out_ref[0, :, cols] = late_ref[pl.ds(0, rows), cols]
        for branch, other, ref in ((1, 2, value_ref), (2, 1, key_ref)):
            x = ref[:, cols].astype(F32)
            one, two = delayed(x, before_ref[other, :, cols].astype(F32))
            value = back * weighted(taps, other, x, one, two)
            new = after_ref[other - 1, :, cols].astype(F32)
            follow = edge * next_featured(taps, other, x, new)
            out_ref[branch, :, cols] = weighted(taps, branch, value, *advanced(value, follow)).astype(BF16)


def summed(x, axis):
    count = lax.axis_size(axis)
    if count & (count - 1):
        return lax.psum(x, axis)
    step = 1
    while step < count:
        x = x + lax.ppermute(x, axis, [(i, i ^ step) for i in range(count)])
        step *= 2
    return x


def layer_step(query_in, key_in, value_in, grad_out, long_filter, short_taps):
    seq = lax.axis_size("seq")
    rows, width = query_in.shape[1:]
    groups = long_filter.shape[2]
    total_rows = rows * seq
    wide = width // groups
    across = LANES * seq
    chunks = width // across
    own_groups = LANES // wide
    chunk_groups = own_groups * seq
    height = 2 * LANES + TILE
    span = math.gcd(SPAN, seq)
    steps = seq // span
    query, key, value, grad = query_in[0], key_in[0], value_in[0], grad_out[0]
    taps = short_taps[0].reshape(9, width)
    last = jnp.stack([query[rows - 2 :], key[rows - 2 :], value[rows - 2 :]])
    before = passed_along(last, "seq", 1)
    top = jnp.stack([key[:2], value[:2], grad[:2]])
    after = passed_along(top, "seq", -1)
    filter_t = long_filter[0].T

    main = pl.BlockSpec((rows, across), lambda c: (0, c))
    sent = pl.pallas_call(
        send_kernel,
        grid=(chunks,),
        in_specs=[
            main, main, main, main,
            pl.BlockSpec((3, 2, across), lambda c: (0, 0, c)),
            pl.BlockSpec((9, across), lambda c: (0, c)),
            pl.BlockSpec((chunk_groups, rows), lambda c: (c, 0)),
        ],
        out_specs=pl.BlockSpec((seq, height, rows), lambda c: (0, c, 0)),
        out_shape=jax.ShapeDtypeStruct((seq, chunks * height, rows), BF16),
        name="send",
    )(query, key, value, grad, before, taps, filter_t)
    arrived = exchange(sent)

    early = {}
    for name, array in (
        ("key", key), ("value", value), ("before", before), ("after", after), ("taps", taps),
    ):
        early[name] = passed_along(array, "pipe", -1)

    layer, passed = None, None
    corr_parts, sum_parts = [], []
    for chunk in range(chunks):
        returned, corr = pl.pallas_call(
            functools.partial(conv_kernel, own_groups, 1.0 / math.sqrt(total_rows * wide)),
            grid=(1,),
            in_specs=[pl.BlockSpec((seq, height, rows), lambda i, chunk=chunk: (0, chunk, 0))],
            out_specs=[
                pl.BlockSpec((seq, height, rows), lambda i: (0, 0, 0)),
                pl.BlockSpec((seq, own_groups, rows), lambda i: (0, 0, 0)),
            ],
            out_shape=[
                jax.ShapeDtypeStruct((seq, height, rows), BF16),
                jax.ShapeDtypeStruct((seq, own_groups, rows), F32),
            ],
            scratch_shapes=[pltpu.VMEM((seq, TILE, LANES), F32)],
            name="conv",
        )(arrived)
        back = exchange(returned)
        corr_parts.append(corr)
        at = lambda i, chunk=chunk: (0, chunk * steps + i)
        at3 = lambda i, chunk=chunk: (0, 0, chunk * steps + i)
        main = pl.BlockSpec((rows, span * LANES), at)
        edge = pl.BlockSpec((3, 2, span * LANES), at3)
        tap_spec = pl.BlockSpec((9, span * LANES), at)
        here = pl.BlockSpec((2 * rows + TILE, span * LANES), lambda i: (0, i))
        has_old = layer is not None
        old = [pl.BlockSpec(memory_space=pl.ANY)] * has_old
        layer, late, sums = pl.pallas_call(
            functools.partial(finish_kernel, 1.0 / math.sqrt(total_rows), has_old),
            grid=(steps,),
            in_specs=[
                main, main, main, main, edge, edge, tap_spec,
                pl.BlockSpec((span, height, rows), lambda i: (i, 0, 0)),
            ]
            + old,
            out_specs=[main, here, pl.BlockSpec((TILE, span * LANES), lambda i: (0, i))],
            out_shape=[
                jax.ShapeDtypeStruct((rows, width), BF16),
                jax.ShapeDtypeStruct((2 * rows + TILE, across), BF16),
                jax.ShapeDtypeStruct((TILE, across), F32),
            ],
            input_output_aliases={8: 0} if has_old else {},
            name="finish",
        )(query, key, value, grad, before, after, taps, back, *([layer] * has_old))
        late = passed_along(late, "pipe", -1)
        sum_parts.append(sums)
        passed = pl.pallas_call(
            functools.partial(apply_kernel, has_old),
            grid=(steps,),
            in_specs=[main, main, edge, edge, tap_spec, here] + old,
            out_specs=pl.BlockSpec((3, rows, span * LANES), at3),
            out_shape=jax.ShapeDtypeStruct((3, rows, width), BF16),
            input_output_aliases={6: 0} if has_old else {},
            name="apply",
        )(
            early["key"], early["value"], early["before"], early["after"], early["taps"], late,
            *([passed] * has_old),
        )

    corr = exchange(jnp.concatenate(corr_parts, axis=1))
    corr = corr.reshape(seq, chunks, own_groups, rows)
    filter_grad = jnp.transpose(corr, (3, 1, 0, 2)).reshape(rows, groups)
    some = [summed(jnp.concatenate(sum_parts[:-1], axis=1), "seq")] if chunks > 1 else []
    some.append(summed(sum_parts[-1], "seq"))
    tap_grads = jnp.concatenate(some, axis=1)[:9].reshape(3, 3, width)
    return (layer[None], passed[None], filter_grad[None], tap_grads[None])


def solution(mesh):
    in_specs = (
        P("pipe", "seq", None),
        P("pipe", "seq", None),
        P("pipe", "seq", None),
        P("pipe", "seq", None),
        P("pipe", "seq", None),
        P("pipe", None, None, None),
    )
    out_specs = (
        P("pipe", "seq", None),
        P("pipe", None, "seq", None),
        P("pipe", "seq", None),
        P("pipe", None, None, None),
    )
    return jax.shard_map(layer_step, mesh=mesh, in_specs=in_specs, out_specs=out_specs, check_vma=False)
```

```python
import functools
import math

import jax
import jax.numpy as jnp
from jax import lax
from jax.experimental import pallas as pl
from jax.experimental.pallas import tpu as pltpu
from jax.sharding import PartitionSpec as P


F32 = jnp.float32
BF16 = jnp.bfloat16
SPAN = 4
TILE = 16
LANES = 128


def passed_along(x, axis, by):
    count = lax.axis_size(axis)
    pairs = [(i, i + by) for i in range(count) if 0 <= i + by < count]
    return lax.ppermute(x, axis, pairs)


def exchange(x):
    return lax.all_to_all(x, "seq", split_axis=0, concat_axis=0, tiled=True)


def dot_nt(left, right):
    return lax.dot_general(
        left, right, (((1,), (1,)), ((), ())), preferred_element_type=F32
    )


def dot_nn(left, right):
    return lax.dot_general(
        left, right, (((1,), (0,)), ((), ())), preferred_element_type=F32
    )


def grid_index(shape, dim):
    return lax.broadcasted_iota(jnp.int32, shape, dim)


def identity(size):
    shape = (size, size)
    return (grid_index(shape, 0) == grid_index(shape, 1)).astype(F32).astype(BF16)


def delayed(x, before, held):
    rows = x.shape[0]
    held[pl.ds(6, 2), :] = before
    held[pl.ds(8, rows), :] = x
    return held[pl.ds(7, rows), :], held[pl.ds(6, rows), :]


def advanced(x, after, held):
    rows = x.shape[0]
    held[pl.ds(0, rows), :] = x
    held[pl.ds(rows, 2), :] = after
    return held[pl.ds(1, rows), :], held[pl.ds(2, rows), :]


def edge_kernel(query_ref, key_ref, value_ref, key_top, value_top, grad_top, last_ref, first_ref):
    for i, ref in enumerate((query_ref, key_ref, value_ref)):
        last_ref[i] = ref[...].astype(F32)[6:8].astype(BF16)
    for i, ref in enumerate((key_top, value_top, grad_top)):
        first_ref[i] = ref[...].astype(F32)[0:2].astype(BF16)


def weighted(taps, branch, x, one, two):
    base = 3 * branch
    out = taps[base : base + 1] * x
    out = out + taps[base + 1 : base + 2] * one
    return out + taps[base + 2 : base + 3] * two


def next_featured(taps, branch, x, new):
    last = x[-8:][6:8]
    one = jnp.concatenate([last[1:2], new[0:1]], axis=0)
    return weighted(taps, branch, new, one, last)


def send_kernel(query_ref, key_ref, value_ref, grad_ref, before_ref, taps_ref, filter_ref, out_ref, held):
    seq, _, _ = out_ref.shape
    all_groups = filter_ref.shape[1]
    count = all_groups // pl.num_programs(0)
    groups = count // seq
    unit = identity(LANES)
    for d in range(seq):
        cols = pl.ds(d * LANES, LANES)
        taps = taps_ref[:, 0, cols]
        feats = []
        for branch, ref in enumerate((query_ref, key_ref, value_ref)):
            x = ref[:, cols].astype(F32)
            one, two = delayed(x, before_ref[branch, :, cols].astype(F32), held.at[d % 2, branch])
            feats.append(weighted(taps, branch, x, one, two))
        product = (feats[1] * feats[2]).astype(BF16)
        scaled = (grad_ref[:, cols].astype(F32) * feats[0]).astype(BF16)
        out_ref[d, pl.ds(0, LANES), :] = dot_nt(unit, product).astype(BF16)
        out_ref[d, pl.ds(LANES, LANES), :] = dot_nt(unit, scaled).astype(BF16)
    shape = (TILE, all_groups)
    rounded = filter_ref[...].astype(BF16)
    for d in range(seq):
        row = grid_index(shape, 0)
        wanted = pl.program_id(0) * count + d * groups + row
        pick = ((row < groups) & (grid_index(shape, 1) == wanted)).astype(F32).astype(BF16)
        out_ref[d, pl.ds(2 * LANES, TILE), :] = dot_nt(pick, rounded).astype(BF16)


def toeplitz_blocks(lines):
    base = [
        pltpu.roll(jnp.broadcast_to(line, (8, LANES)), 0, 1, stride=1, stride_axis=0)
        for line in lines
    ]
    lane = grid_index((8, LANES), 1)
    sub = grid_index((8, LANES), 0)
    zero = jnp.zeros((8, LANES), F32)
    parts = [[] for _ in lines]
    for m in range(LANES // 8):
        below = zero
        for k, start in enumerate(base):
            turned = pltpu.roll(start, 8 * m, 1) if m else start
            parts[k].append(jnp.where(lane >= sub + 8 * m, turned, below))
            below = turned
    return [jnp.concatenate(part, axis=0).astype(BF16) for part in parts]


def diagonal_sums(cross, blocks):
    parts = [cross[:, k * LANES : (k + 1) * LANES] for k in range(blocks)]
    rows = LANES
    while rows > 8:
        half = rows // 2
        lane = grid_index((half, LANES), 1)
        turned = [pltpu.roll(part[half:rows], LANES - half, 1) for part in parts]
        turned.append(jnp.zeros((half, LANES), F32))
        parts = [
            parts[k][:half] + jnp.where(lane < LANES - half, turned[k], turned[k + 1])
            for k in range(blocks)
        ]
        rows = half
    lane = grid_index((8, LANES), 1)
    sub = grid_index((8, LANES), 0)
    turned = [pltpu.roll(part, LANES - 7, 1, stride=1, stride_axis=0) for part in parts]
    turned.append(jnp.zeros((8, LANES), F32))
    keep = lane < sub + (LANES - 7)
    return [
        jnp.sum(jnp.where(keep, turned[k], turned[k + 1]), axis=0, keepdims=True)
        for k in range(blocks)
    ]


def conv_kernel(groups, chunk, scale, in_ref, out_ref, corr, taps, even_taps, odd_taps, even_cross, odd_cross):
    blocks = in_ref.shape[0]
    wide = LANES // groups
    rows = blocks * wide
    start = chunk * (2 * LANES + TILE)
    lane = grid_index((LANES, LANES), 1)
    sub = grid_index((LANES, LANES), 0)
    flipped = (sub // 8) * 8 + 7 - sub % 8
    flip = (lane == flipped).astype(F32).astype(BF16)
    taps[...] = in_ref[:, pl.ds(start + 2 * LANES, TILE), :].astype(F32)
    odd_cross[...] = jnp.zeros(odd_cross.shape, F32)

    def spread(g, table):
        lines = [taps[k, pl.ds(g, 1), :] for k in range(blocks)]
        for k, block in enumerate(toeplitz_blocks(lines)):
            table[:, pl.ds(k * LANES, LANES)] = block

    def multiply(g, table, cross):
        at = pl.multiple_of(g * wide, wide)
        first = in_ref[:, pl.ds(start + at, wide), :].reshape(rows, LANES)
        second = in_ref[:, pl.ds(start + LANES + at, wide), :].reshape(rows, LANES)
        shifted, ahead = [first], [second]
        for k in range(1, blocks):
            gap = jnp.zeros((wide * k, LANES), BF16)
            shifted.append(jnp.concatenate([gap, first[: rows - wide * k]], axis=0))
            ahead.append(jnp.concatenate([second[wide * k :], gap], axis=0))
        ahead = jnp.concatenate(ahead, axis=1)
        stacked = [table[:, pl.ds(k * LANES, LANES)] for k in range(blocks)]
        conv = dot_nn(jnp.concatenate(shifted, axis=1), jnp.concatenate(stacked, axis=0))
        back = dot_nt(ahead, table[...])
        out_ref[:, pl.ds(at, wide), :] = conv.astype(BF16).reshape(blocks, wide, LANES)
        out_ref[:, pl.ds(LANES + at, wide), :] = back.astype(BF16).reshape(blocks, wide, LANES)
        cross[...] = dot_nn(dot_nt(flip, first).astype(BF16), ahead)

    def collect(g, cross):
        for k, line in enumerate(diagonal_sums(cross[...], blocks)):
            corr[k, pl.ds(g, 1), :] = line * scale

    spread(0, even_taps)

    def two_groups(step, carry):
        g = 2 * step
        spread(g + 1, odd_taps)
        multiply(g, even_taps, even_cross)
        collect(jnp.maximum(g - 1, 0), odd_cross)
        spread(jnp.minimum(g + 2, groups - 1), even_taps)
        multiply(g + 1, odd_taps, odd_cross)
        collect(g, even_cross)
        return carry

    lax.fori_loop(0, groups // 2, two_groups, 0)
    collect(groups - 1, odd_cross)
    pick_row = grid_index((TILE, 2 * LANES), 0)
    pick_lane = grid_index((TILE, 2 * LANES), 1)
    wanted = (pick_row // 2) * LANES + pick_row % 2
    pick = ((pick_row < 4) & (pick_lane == wanted)).astype(F32).astype(BF16)
    for a in range(blocks):
        if a + 1 < blocks:
            both = [out_ref[a + 1, pl.ds(0, LANES), :], out_ref[a + 1, pl.ds(LANES, LANES), :]]
            line = dot_nt(pick, jnp.concatenate(both, axis=1)).astype(BF16)
        else:
            line = jnp.zeros((TILE, LANES), BF16)
        out_ref[a, pl.ds(2 * LANES, TILE), :] = line
        full = corr[a]
        high = full.astype(BF16).astype(F32)
        pair = jnp.concatenate([high, full - high], axis=0).astype(BF16)
        out_ref[a, pl.ds(2 * LANES + TILE, 2 * groups), :] = pair


def finish_kernel(
    scale, has_old, query_ref, key_ref, value_ref, grad_ref, before_ref, after_ref, taps_ref, in_ref, *refs
):
    layer_ref, late_ref, sums_ref, corr_ref, held = refs[3:] if has_old else refs
    groups = corr_ref.shape[0] // in_ref.shape[0]
    rows = query_ref.shape[0]
    unit = identity(LANES)
    for part in range(in_ref.shape[0]):
        cols = pl.ds(part * LANES, LANES)
        taps = taps_ref[:, 0, cols]
        conv = dot_nt(unit, in_ref[part, pl.ds(0, LANES), :])
        back = dot_nt(unit, in_ref[part, pl.ds(LANES, LANES), :])
        edge = in_ref[part, pl.ds(2 * LANES, TILE), :].astype(F32)
        grad = grad_ref[:, cols].astype(F32)
        lines = []

        def raw_of(branch, ref):
            x = ref[:, cols].astype(F32)
            before = before_ref[branch, :, cols].astype(F32)
            return (x,) + delayed(x, before, held.at[part % 2, branch])

        def tap_lines(value, raw):
            for shifted in raw:
                lines.append(jnp.sum(value * shifted, axis=0, keepdims=True) * scale)

        raw = raw_of(0, query_ref)
        layer_ref[:, cols] = (weighted(taps, 0, *raw) * conv).astype(BF16)
        value = grad * conv
        tap_lines(value, raw)
        follow = after_ref[2, :, cols].astype(F32) * edge[0:2]
        total = weighted(taps, 0, value, *advanced(value, follow, held.at[part % 2, 3]))
        late_ref[pl.ds(0, rows), cols] = total.astype(BF16)
        key_raw = raw_of(1, key_ref)
        value_raw = raw_of(2, value_ref)
        tap_lines(back * weighted(taps, 2, *value_raw), key_raw)
        tap_lines(back * weighted(taps, 1, *key_raw), value_raw)
        late_ref[pl.ds(rows, rows), cols] = back.astype(BF16)
        tail = jnp.concatenate([edge[2:4], jnp.zeros((TILE - 2, LANES), F32)], axis=0)
        late_ref[pl.ds(2 * rows, TILE), cols] = tail.astype(BF16)
        for index, line in enumerate(lines):
            sums_ref[index, :, cols] = line
        pair = in_ref[part, pl.ds(2 * LANES + TILE, 2 * groups), :].astype(F32)
        corr_ref[pl.ds(part * groups, groups), :] = pair[:groups] + pair[groups:]


def apply_kernel(has_old, key_ref, value_ref, before_ref, after_ref, taps_ref, late_ref, *refs):
    out_ref, held = refs[1:] if has_old else refs
    rows, width = key_ref.shape
    for part in range(width // LANES):
        cols = pl.ds(part * LANES, LANES)
        taps = taps_ref[:, 0, cols]
        back = late_ref[pl.ds(rows, rows), cols].astype(F32)
        edge = late_ref[pl.ds(2 * rows, TILE), cols].astype(F32)[0:2]
        out_ref[0, :, cols] = late_ref[pl.ds(0, rows), cols]
        for branch, other, ref in ((1, 2, value_ref), (2, 1, key_ref)):
            x = ref[:, cols].astype(F32)
            one, two = delayed(x, before_ref[other, :, cols].astype(F32), held.at[part % 2, branch - 1])
            value = back * weighted(taps, other, x, one, two)
            new = after_ref[other - 1, :, cols].astype(F32)
            follow = edge * next_featured(taps, other, x, new)
            one, two = advanced(value, follow, held.at[part % 2, branch + 1])
            out_ref[branch, :, cols] = weighted(taps, branch, value, one, two).astype(BF16)


def summed(x, axis):
    count = lax.axis_size(axis)
    if count & (count - 1):
        return lax.psum(x, axis)
    for bit in range(count.bit_length() - 1):
        x = x + lax.ppermute(x, axis, [(i, i ^ (1 << bit)) for i in range(count)])
    return x


def layer_step(query_in, key_in, value_in, grad_out, long_filter, short_taps):
    seq = lax.axis_size("seq")
    rows, width = query_in.shape[1:]
    groups = long_filter.shape[2]
    total_rows = rows * seq
    wide = width // groups
    across = LANES * seq
    chunks = width // across
    own_groups = LANES // wide
    height = 2 * LANES + TILE
    back_height = height + 2 * own_groups
    span = math.gcd(SPAN, seq)
    steps = seq // span
    query, key, value, grad = query_in[0], key_in[0], value_in[0], grad_out[0]
    taps = short_taps[0].reshape(9, 1, width)
    low = pl.BlockSpec((8, width), lambda i: (rows // 8 - 1, 0))
    high = pl.BlockSpec((8, width), lambda i: (0, 0))
    two_rows = pl.BlockSpec((3, 2, width), lambda i: (0, 0, 0))
    last, top = pl.pallas_call(
        edge_kernel,
        grid=(1,),
        in_specs=[low, low, low, high, high, high],
        out_specs=[two_rows, two_rows],
        out_shape=[jax.ShapeDtypeStruct((3, 2, width), BF16)] * 2,
        name="edges",
    )(query, key, value, key, value, grad)
    before = passed_along(last, "seq", 1)
    after = passed_along(top, "seq", -1)

    main = pl.BlockSpec((rows, across), lambda c: (0, c))
    sent = pl.pallas_call(
        send_kernel,
        grid=(chunks,),
        in_specs=[
            main, main, main, main,
            pl.BlockSpec((3, 2, across), lambda c: (0, 0, c)),
            pl.BlockSpec((9, 1, across), lambda c: (0, 0, c)),
            pl.BlockSpec((rows, groups), lambda c: (0, 0)),
        ],
        out_specs=pl.BlockSpec((seq, height, rows), lambda c: (0, c, 0)),
        out_shape=jax.ShapeDtypeStruct((seq, chunks * height, rows), BF16),
        scratch_shapes=[pltpu.VMEM((2, 3, rows + 8, LANES), F32)],
        name="send",
    )(query, key, value, grad, before, taps, long_filter[0])
    arrived = exchange(sent)

    early = {}
    for name, array in (
        ("key", key), ("value", value), ("before", before), ("after", after), ("taps", taps),
    ):
        early[name] = passed_along(array, "pipe", -1)

    layer, passed, tap_sums, corr = None, None, None, None
    for chunk in range(chunks):
        returned = pl.pallas_call(
            functools.partial(conv_kernel, own_groups, chunk, 1.0 / math.sqrt(total_rows * wide)),
            in_specs=[pl.BlockSpec(memory_space=pltpu.VMEM)],
            out_specs=pl.BlockSpec(memory_space=pltpu.VMEM),
            out_shape=jax.ShapeDtypeStruct((seq, back_height, rows), BF16),
            scratch_shapes=[pltpu.VMEM((seq, own_groups, LANES), F32), pltpu.VMEM((seq, TILE, LANES), F32)]
            + [pltpu.VMEM((LANES, total_rows), BF16)] * 2
            + [pltpu.VMEM((LANES, total_rows), F32)] * 2,
            name="conv",
            compiler_params=pltpu.CompilerParams(vmem_limit_bytes=24 * 2**20),
        )(arrived)
        back = exchange(returned)
        at = lambda i, chunk=chunk: (0, chunk * steps + i)
        at3 = lambda i, chunk=chunk: (0, 0, chunk * steps + i)
        main = pl.BlockSpec((rows, span * LANES), at)
        edge = pl.BlockSpec((3, 2, span * LANES), at3)
        tap_spec = pl.BlockSpec((9, 1, span * LANES), at3)
        here = pl.BlockSpec((2 * rows + TILE, span * LANES), lambda i: (0, i))
        has_old = layer is not None
        old = [pl.BlockSpec(memory_space=pl.ANY)] * has_old
        layer, late, tap_sums, corr = pl.pallas_call(
            functools.partial(finish_kernel, 1.0 / math.sqrt(total_rows), has_old),
            grid=(steps,),
            in_specs=[
                main, main, main, main, edge, edge, tap_spec,
                pl.BlockSpec((span, back_height, rows), lambda i: (i, 0, 0)),
            ]
            + old * 3,
            out_specs=[
                main, here, tap_spec,
                pl.BlockSpec((span * own_groups, rows), lambda i, chunk=chunk: (chunk * steps + i, 0)),
            ],
            out_shape=[
                jax.ShapeDtypeStruct((rows, width), BF16),
                jax.ShapeDtypeStruct((2 * rows + TILE, across), BF16),
                jax.ShapeDtypeStruct((9, 1, width), F32),
                jax.ShapeDtypeStruct((groups, rows), F32),
            ],
            input_output_aliases={8: 0, 9: 2, 10: 3} if has_old else {},
            scratch_shapes=[pltpu.VMEM((2, 4, rows + 8, LANES), F32)],
            name="finish",
        )(query, key, value, grad, before, after, taps, back, *([layer, tap_sums, corr] if has_old else []))
        late = passed_along(late, "pipe", -1)
        passed = pl.pallas_call(
            functools.partial(apply_kernel, has_old),
            grid=(steps,),
            in_specs=[main, main, edge, edge, tap_spec, here] + old,
            out_specs=pl.BlockSpec((3, rows, span * LANES), at3),
            out_shape=jax.ShapeDtypeStruct((3, rows, width), BF16),
            input_output_aliases={6: 0} if has_old else {},
            scratch_shapes=[pltpu.VMEM((2, 4, rows + 8, LANES), F32)],
            name="apply",
        )(
            early["key"], early["value"], early["before"], early["after"], early["taps"], late,
            *([passed] * has_old),
        )

    filter_grad = corr.T
    tap_grads = summed(tap_sums, "seq").reshape(3, 3, width)
    return (layer[None], passed[None], filter_grad[None], tap_grads[None])


def solution(mesh):
    in_specs = (
        P("pipe", "seq", None),
        P("pipe", "seq", None),
        P("pipe", "seq", None),
        P("pipe", "seq", None),
        P("pipe", "seq", None),
        P("pipe", None, None, None),
    )
    out_specs = (
        P("pipe", "seq", None),
        P("pipe", None, "seq", None),
        P("pipe", "seq", None),
        P("pipe", None, None, None),
    )
    return jax.shard_map(layer_step, mesh=mesh, in_specs=in_specs, out_specs=out_specs, check_vma=False)
```

```python
import functools
import math

import jax
import jax.numpy as jnp
from jax import lax
from jax.experimental import pallas as pl
from jax.experimental.pallas import tpu as pltpu
from jax.sharding import PartitionSpec as P


F32 = jnp.float32
BF16 = jnp.bfloat16
FINISH_SPAN = 4
APPLY_SPAN = 4
TILE = 16
LANES = 128


def passed_along(x, axis, by):
    count = lax.axis_size(axis)
    pairs = [(i, i + by) for i in range(count) if 0 <= i + by < count]
    return lax.ppermute(x, axis, pairs)


def exchange(x):
    return lax.all_to_all(x, "seq", split_axis=0, concat_axis=0, tiled=True)


def dot_nt(left, right):
    return lax.dot_general(
        left, right, (((1,), (1,)), ((), ())), preferred_element_type=F32
    )


def dot_nn(left, right):
    return lax.dot_general(
        left, right, (((1,), (0,)), ((), ())), preferred_element_type=F32
    )


def grid_index(shape, dim):
    return lax.broadcasted_iota(jnp.int32, shape, dim)


def identity(size):
    shape = (size, size)
    return (grid_index(shape, 0) == grid_index(shape, 1)).astype(F32).astype(BF16)


def delayed(x, before, held):
    rows = x.shape[0]
    held[pl.ds(6, 2), :] = before
    held[pl.ds(8, rows), :] = x
    return held[pl.ds(7, rows), :], held[pl.ds(6, rows), :]


def advanced(x, after, held):
    rows = x.shape[0]
    held[pl.ds(0, rows), :] = x
    held[pl.ds(rows, 2), :] = after
    return held[pl.ds(1, rows), :], held[pl.ds(2, rows), :]


def edge_kernel(query_ref, key_ref, value_ref, key_top, value_top, grad_top, last_ref, first_ref):
    for i, ref in enumerate((query_ref, key_ref, value_ref)):
        last_ref[i] = ref[...].astype(F32)[6:8].astype(BF16)
    for i, ref in enumerate((key_top, value_top, grad_top)):
        first_ref[i] = ref[...].astype(F32)[0:2].astype(BF16)


def weighted(taps, branch, x, one, two):
    base = 3 * branch
    out = taps[base : base + 1] * x
    out = out + taps[base + 1 : base + 2] * one
    return out + taps[base + 2 : base + 3] * two


def next_featured(taps, branch, x, new):
    last = x[-8:][6:8]
    one = jnp.concatenate([last[1:2], new[0:1]], axis=0)
    return weighted(taps, branch, new, one, last)


def partner(rank, step, count, sign):
    if count & (count - 1):
        return lax.rem(rank + sign * step + count, jnp.int32(count))
    return rank ^ step


def send_kernel(
    first_chunk, chunks, spread, rank_ref, query_ref, key_ref, value_ref, grad_ref, before_ref, taps_ref, filter_ref,
    *refs,
):
    outs, held = refs[:-1], refs[-1]
    seq = query_ref.shape[1] // LANES
    all_groups = filter_ref.shape[1]
    count = all_groups // chunks
    groups = count // seq
    unit = identity(LANES)
    rounded = filter_ref[...].astype(BF16)
    row = grid_index((TILE, all_groups), 0)
    column = grid_index((TILE, all_groups), 1)
    for step in range(seq):
        d = partner(rank_ref[0], step, seq, 1) if spread else step
        out = outs[step] if spread else outs[0].at[step]
        cols = pl.ds(pl.multiple_of(d * LANES, LANES) if spread else d * LANES, LANES)
        taps = taps_ref[:, 0, cols]
        feats = []
        for branch, ref in enumerate((query_ref, key_ref, value_ref)):
            x = ref[:, cols].astype(F32)
            one, two = delayed(x, before_ref[branch, :, cols].astype(F32), held.at[step % 2, branch])
            feats.append(weighted(taps, branch, x, one, two))
        product = (feats[1] * feats[2]).astype(BF16)
        scaled = (grad_ref[:, cols].astype(F32) * feats[0]).astype(BF16)
        out[pl.ds(0, LANES), :] = dot_nt(unit, product).astype(BF16)
        out[pl.ds(LANES, LANES), :] = dot_nt(unit, scaled).astype(BF16)
        wanted = (first_chunk + pl.program_id(0)) * count + d * groups + row
        pick = ((row < groups) & (column == wanted)).astype(F32).astype(BF16)
        out[pl.ds(2 * LANES, TILE), :] = dot_nt(pick, rounded).astype(BF16)


def toeplitz_blocks(lines):
    base = [
        pltpu.roll(jnp.broadcast_to(line, (8, LANES)), 0, 1, stride=1, stride_axis=0)
        for line in lines
    ]
    lane = grid_index((8, LANES), 1)
    sub = grid_index((8, LANES), 0)
    zero = jnp.zeros((8, LANES), F32)
    parts = [[] for _ in lines]
    for m in range(LANES // 8):
        below = zero
        for k, start in enumerate(base):
            turned = pltpu.roll(start, 8 * m, 1) if m else start
            parts[k].append(jnp.where(lane >= sub + 8 * m, turned, below))
            below = turned
    return [jnp.concatenate(part, axis=0).astype(BF16) for part in parts]


def diagonal_sums(cross, blocks):
    parts = [cross[:, k * LANES : (k + 1) * LANES] for k in range(blocks)]
    rows = LANES
    while rows > 8:
        half = rows // 2
        lane = grid_index((half, LANES), 1)
        turned = [pltpu.roll(part[half:rows], LANES - half, 1) for part in parts]
        turned.append(jnp.zeros((half, LANES), F32))
        parts = [
            parts[k][:half] + jnp.where(lane < LANES - half, turned[k], turned[k + 1])
            for k in range(blocks)
        ]
        rows = half
    lane = grid_index((8, LANES), 1)
    sub = grid_index((8, LANES), 0)
    turned = [pltpu.roll(part, LANES - 7, 1, stride=1, stride_axis=0) for part in parts]
    turned.append(jnp.zeros((8, LANES), F32))
    keep = lane < sub + (LANES - 7)
    return [
        jnp.sum(jnp.where(keep, turned[k], turned[k + 1]), axis=0, keepdims=True)
        for k in range(blocks)
    ]


def conv_kernel(groups, chunk, count, scale, *refs):
    if chunk is None:
        in_ref = refs[0]
        refs = refs[1:]
    else:
        in_ref = refs[-1]
        for step in range(count):
            in_ref[partner(refs[0][0], step, count, -1)] = refs[1 + step][...]
        refs = refs[1 + count : -1]
    out_ref, corr, taps, even_taps, odd_taps, even_cross, odd_cross = refs
    blocks = in_ref.shape[0]
    wide = LANES // groups
    rows = blocks * wide
    lane = grid_index((LANES, LANES), 1)
    sub = grid_index((LANES, LANES), 0)
    flipped = (sub // 8) * 8 + 7 - sub % 8
    flip = (lane == flipped).astype(F32).astype(BF16)
    taps[...] = in_ref[:, pl.ds(2 * LANES, TILE), :].astype(F32)
    odd_cross[...] = jnp.zeros(odd_cross.shape, F32)

    def spread(g, table):
        lines = [taps[k, pl.ds(g, 1), :] for k in range(blocks)]
        for k, block in enumerate(toeplitz_blocks(lines)):
            table[:, pl.ds(k * LANES, LANES)] = block

    def multiply(g, table, cross):
        at = pl.multiple_of(g * wide, wide)
        first = in_ref[:, pl.ds(at, wide), :].reshape(rows, LANES)
        second = in_ref[:, pl.ds(LANES + at, wide), :].reshape(rows, LANES)
        shifted, ahead = [first], [second]
        for k in range(1, blocks):
            gap = jnp.zeros((wide * k, LANES), BF16)
            shifted.append(jnp.concatenate([gap, first[: rows - wide * k]], axis=0))
            ahead.append(jnp.concatenate([second[wide * k :], gap], axis=0))
        ahead = jnp.concatenate(ahead, axis=1)
        stacked = [table[:, pl.ds(k * LANES, LANES)] for k in range(blocks)]
        conv = dot_nn(jnp.concatenate(shifted, axis=1), jnp.concatenate(stacked, axis=0))
        back = dot_nt(ahead, table[...])
        out_ref[:, pl.ds(at, wide), :] = conv.astype(BF16).reshape(blocks, wide, LANES)
        out_ref[:, pl.ds(LANES + at, wide), :] = back.astype(BF16).reshape(blocks, wide, LANES)
        cross[...] = dot_nn(dot_nt(flip, first).astype(BF16), ahead)

    def collect(g, cross):
        for k, line in enumerate(diagonal_sums(cross[...], blocks)):
            corr[k, pl.ds(g, 1), :] = line * scale

    spread(0, even_taps)

    def two_groups(step, carry):
        g = 2 * step
        spread(g + 1, odd_taps)
        multiply(g, even_taps, even_cross)
        collect(jnp.maximum(g - 1, 0), odd_cross)
        spread(jnp.minimum(g + 2, groups - 1), even_taps)
        multiply(g + 1, odd_taps, odd_cross)
        collect(g, even_cross)
        return carry

    lax.fori_loop(0, groups // 2, two_groups, 0)
    collect(groups - 1, odd_cross)
    pick_row = grid_index((TILE, 2 * LANES), 0)
    pick_lane = grid_index((TILE, 2 * LANES), 1)
    wanted = (pick_row // 2) * LANES + pick_row % 2
    pick = ((pick_row < 4) & (pick_lane == wanted)).astype(F32).astype(BF16)
    for a in range(blocks):
        if a + 1 < blocks:
            both = [out_ref[a + 1, pl.ds(0, LANES), :], out_ref[a + 1, pl.ds(LANES, LANES), :]]
            line = dot_nt(pick, jnp.concatenate(both, axis=1)).astype(BF16)
        else:
            line = jnp.zeros((TILE, LANES), BF16)
        out_ref[a, pl.ds(2 * LANES, TILE), :] = line
        full = corr[a]
        high = full.astype(BF16).astype(F32)
        pair = jnp.concatenate([high, full - high], axis=0).astype(BF16)
        out_ref[a, pl.ds(2 * LANES + TILE, 2 * groups), :] = pair


def finish_kernel(
    scale, has_old, query_ref, key_ref, value_ref, grad_ref, before_ref, after_ref, taps_ref, in_ref, *refs
):
    layer_ref, late_ref, sums_ref, corr_ref, held = refs[3:] if has_old else refs
    groups = corr_ref.shape[0] // in_ref.shape[0]
    rows = query_ref.shape[0]
    unit = identity(LANES)
    for part in range(in_ref.shape[0]):
        cols = pl.ds(part * LANES, LANES)
        taps = taps_ref[:, 0, cols]
        conv = dot_nt(unit, in_ref[part, pl.ds(0, LANES), :])
        back = dot_nt(unit, in_ref[part, pl.ds(LANES, LANES), :])
        edge = in_ref[part, pl.ds(2 * LANES, TILE), :].astype(F32)
        grad = grad_ref[:, cols].astype(F32)
        lines = []

        def raw_of(branch, ref):
            x = ref[:, cols].astype(F32)
            before = before_ref[branch, :, cols].astype(F32)
            return (x,) + delayed(x, before, held.at[part % 2, branch])

        def tap_lines(value, raw):
            for shifted in raw:
                lines.append(jnp.sum(value * shifted, axis=0, keepdims=True) * scale)

        raw = raw_of(0, query_ref)
        layer_ref[:, cols] = (weighted(taps, 0, *raw) * conv).astype(BF16)
        value = grad * conv
        tap_lines(value, raw)
        follow = after_ref[2, :, cols].astype(F32) * edge[0:2]
        total = weighted(taps, 0, value, *advanced(value, follow, held.at[part % 2, 3]))
        late_ref[pl.ds(0, rows), cols] = total.astype(BF16)
        key_raw = raw_of(1, key_ref)
        value_raw = raw_of(2, value_ref)
        tap_lines(back * weighted(taps, 2, *value_raw), key_raw)
        tap_lines(back * weighted(taps, 1, *key_raw), value_raw)
        late_ref[pl.ds(rows, rows), cols] = back.astype(BF16)
        tail = jnp.concatenate([edge[2:4], jnp.zeros((6, LANES), F32)], axis=0)
        late_ref[pl.ds(2 * rows, 8), cols] = tail.astype(BF16)
        for index, line in enumerate(lines):
            sums_ref[index, :, cols] = line
        pair = in_ref[part, pl.ds(2 * LANES + TILE, 2 * groups), :].astype(F32)
        corr_ref[pl.ds(part * groups, groups), :] = pair[:groups] + pair[groups:]


def apply_kernel(has_old, key_ref, value_ref, edges_ref, taps_ref, late_ref, *refs):
    out_ref, held = refs[1:] if has_old else refs
    rows, width = key_ref.shape
    for part in range(width // LANES):
        cols = pl.ds(part * LANES, LANES)
        taps = taps_ref[:, 0, cols]
        back = late_ref[pl.ds(rows, rows), cols].astype(F32)
        edge = late_ref[pl.ds(2 * rows, 8), cols].astype(F32)[0:2]
        out_ref[0, :, cols] = late_ref[pl.ds(0, rows), cols]
        for branch, ref in ((0, value_ref), (1, key_ref)):
            other = 1 - branch
            x = ref[:, cols].astype(F32)
            one, two = delayed(x, edges_ref[other, :, cols].astype(F32), held.at[part % 2, branch])
            value = back * weighted(taps, other, x, one, two)
            new = edges_ref[2 + other, :, cols].astype(F32)
            follow = edge * next_featured(taps, other, x, new)
            one, two = advanced(value, follow, held.at[part % 2, branch + 2])
            out_ref[branch + 1, :, cols] = weighted(taps, branch, value, one, two).astype(BF16)


def summed(x, axis):
    count = lax.axis_size(axis)
    if count & (count - 1):
        return lax.psum(x, axis)
    for bit in range(count.bit_length() - 1):
        x = x + lax.ppermute(x, axis, [(i, i ^ (1 << bit)) for i in range(count)])
    return x


def batches(chunks):
    return [(0, 1), (1, chunks)] if chunks > 1 else [(0, 1)]


def layer_step(query_in, key_in, value_in, grad_out, long_filter, short_taps):
    seq = lax.axis_size("seq")
    rows, width = query_in.shape[1:]
    groups = long_filter.shape[2]
    total_rows = rows * seq
    wide = width // groups
    across = LANES * seq
    chunks = width // across
    own_groups = LANES // wide
    height = 2 * LANES + TILE
    back_height = height + 2 * own_groups
    span = math.gcd(FINISH_SPAN, seq)
    steps = seq // span
    last_span = math.gcd(APPLY_SPAN, seq)
    last_steps = seq // last_span
    query, key, value, grad = query_in[0], key_in[0], value_in[0], grad_out[0]
    taps = short_taps[0].reshape(9, 1, width)
    low = pl.BlockSpec((8, width), lambda i: (rows // 8 - 1, 0))
    high = pl.BlockSpec((8, width), lambda i: (0, 0))
    two_rows = pl.BlockSpec((3, 2, width), lambda i: (0, 0, 0))
    last, top = pl.pallas_call(
        edge_kernel,
        grid=(1,),
        in_specs=[low, low, low, high, high, high],
        out_specs=[two_rows, two_rows],
        out_shape=[jax.ShapeDtypeStruct((3, 2, width), BF16)] * 2,
        name="edges",
    )(query, key, value, key, value, grad)
    before = passed_along(last, "seq", 1)
    after = passed_along(top, "seq", -1)

    rank = lax.axis_index("seq").astype(jnp.int32).reshape(1)
    scalar = pl.BlockSpec(memory_space=pltpu.SMEM)
    arrived = []
    for part, (low, high) in enumerate(batches(chunks)):
        main = pl.BlockSpec((rows, across), lambda c, low=low: (0, low + c))
        if part:
            out_specs = [pl.BlockSpec((height, rows), lambda c: (c, 0))] * seq
            out_shape = [jax.ShapeDtypeStruct(((high - low) * height, rows), BF16)] * seq
        else:
            out_specs = [pl.BlockSpec((seq, height, rows), lambda c: (0, c, 0))]
            out_shape = [jax.ShapeDtypeStruct((seq, height, rows), BF16)]
        sent = pl.pallas_call(
            functools.partial(send_kernel, low, chunks, part > 0),
            grid=(high - low,),
            in_specs=[
                scalar, main, main, main, main,
                pl.BlockSpec((3, 2, across), lambda c, low=low: (0, 0, low + c)),
                pl.BlockSpec((9, 1, across), lambda c, low=low: (0, 0, low + c)),
                pl.BlockSpec((rows, groups), lambda c: (0, 0)),
            ],
            out_specs=out_specs,
            out_shape=out_shape,
            scratch_shapes=[pltpu.VMEM((2, 3, rows + 8, LANES), F32)],
            name="send",
        )(rank, query, key, value, grad, before, taps, long_filter[0])
        if not part:
            arrived.append((None, (exchange(sent[0]),)))
            continue
        there = [sent[0]]
        for step in range(1, seq):
            pairs = [(i, i ^ step if seq & (seq - 1) == 0 else (i + step) % seq) for i in range(seq)]
            there.append(lax.ppermute(sent[step], "seq", pairs))
        arrived += [(chunk, (rank, *there)) for chunk in range(high - low)]

    early = {}
    edges = jnp.concatenate([before[1:], after[:2]], axis=0)
    for name, array in (("key", key), ("value", value), ("edges", edges), ("taps", taps[3:])):
        early[name] = passed_along(array, "pipe", -1)

    layer, passed, tap_sums, corr = None, None, None, None
    for chunk in range(chunks):
        place, there = arrived[chunk]
        returned = pl.pallas_call(
            functools.partial(conv_kernel, own_groups, place, seq, 1.0 / math.sqrt(total_rows * wide)),
            grid=(1,),
            in_specs=[pl.BlockSpec((seq, height, rows), lambda i: (0, 0, 0))]
            if place is None
            else [scalar] + [pl.BlockSpec((height, rows), lambda i, place=place: (place, 0))] * seq,
            out_specs=pl.BlockSpec((seq, back_height, rows), lambda i: (0, 0, 0)),
            out_shape=jax.ShapeDtypeStruct((seq, back_height, rows), BF16),
            scratch_shapes=[pltpu.VMEM((seq, own_groups, LANES), F32), pltpu.VMEM((seq, TILE, LANES), F32)]
            + [pltpu.VMEM((LANES, total_rows), BF16)] * 2
            + [pltpu.VMEM((LANES, total_rows), F32)] * 2
            + [pltpu.VMEM((seq, height, LANES), BF16)] * (place is not None),
            name="conv",
            compiler_params=pltpu.CompilerParams(vmem_limit_bytes=24 * 2**20),
        )(*there)
        back = exchange(returned)
        at = lambda i, chunk=chunk: (0, chunk * steps + i)
        at3 = lambda i, chunk=chunk: (0, 0, chunk * steps + i)
        last = lambda i, chunk=chunk: (0, chunk * last_steps + i)
        last3 = lambda i, chunk=chunk: (0, 0, chunk * last_steps + i)
        main = pl.BlockSpec((rows, span * LANES), at)
        edge = pl.BlockSpec((3, 2, span * LANES), at3)
        tap_spec = pl.BlockSpec((9, 1, span * LANES), at3)
        here = pl.BlockSpec((2 * rows + 8, span * LANES), lambda i: (0, i))
        has_old = layer is not None
        old = [pl.BlockSpec(memory_space=pl.ANY)] * has_old
        layer, late, tap_sums, corr = pl.pallas_call(
            functools.partial(finish_kernel, 1.0 / math.sqrt(total_rows), has_old),
            grid=(steps,),
            in_specs=[
                main, main, main, main, edge, edge, tap_spec,
                pl.BlockSpec((span, back_height, rows), lambda i: (i, 0, 0)),
            ]
            + old * 3,
            out_specs=[
                main, here, tap_spec,
                pl.BlockSpec((span * own_groups, rows), lambda i, chunk=chunk: (chunk * steps + i, 0)),
            ],
            out_shape=[
                jax.ShapeDtypeStruct((rows, width), BF16),
                jax.ShapeDtypeStruct((2 * rows + 8, across), BF16),
                jax.ShapeDtypeStruct((9, 1, width), F32),
                jax.ShapeDtypeStruct((groups, rows), F32),
            ],
            input_output_aliases={8: 0, 9: 2, 10: 3} if has_old else {},
            scratch_shapes=[pltpu.VMEM((2, 4, rows + 8, LANES), F32)],
            name="finish",
        )(query, key, value, grad, before, after, taps, back, *([layer, tap_sums, corr] if has_old else []))
        late = passed_along(late, "pipe", -1)
        passed = pl.pallas_call(
            functools.partial(apply_kernel, has_old),
            grid=(last_steps,),
            in_specs=[
                pl.BlockSpec((rows, last_span * LANES), last),
                pl.BlockSpec((rows, last_span * LANES), last),
                pl.BlockSpec((4, 2, last_span * LANES), last3),
                pl.BlockSpec((6, 1, last_span * LANES), last3),
                pl.BlockSpec((2 * rows + 8, last_span * LANES), lambda i: (0, i)),
            ]
            + old,
            out_specs=pl.BlockSpec((3, rows, last_span * LANES), last3),
            out_shape=jax.ShapeDtypeStruct((3, rows, width), BF16),
            input_output_aliases={5: 0} if has_old else {},
            scratch_shapes=[pltpu.VMEM((2, 4, rows + 8, LANES), F32)],
            name="apply",
            compiler_params=pltpu.CompilerParams(vmem_limit_bytes=24 * 2**20),
        )(
            early["key"], early["value"], early["edges"], early["taps"], late,
            *([passed] * has_old),
        )

    filter_grad = corr.T
    tap_grads = summed(tap_sums, "seq").reshape(3, 3, width)
    return (layer[None], passed[None], filter_grad[None], tap_grads[None])


def solution(mesh):
    in_specs = (
        P("pipe", "seq", None),
        P("pipe", "seq", None),
        P("pipe", "seq", None),
        P("pipe", "seq", None),
        P("pipe", "seq", None),
        P("pipe", None, None, None),
    )
    out_specs = (
        P("pipe", "seq", None),
        P("pipe", None, "seq", None),
        P("pipe", "seq", None),
        P("pipe", None, None, None),
    )
    return jax.shard_map(layer_step, mesh=mesh, in_specs=in_specs, out_specs=out_specs, check_vma=False)
```

```python
import functools
import math

import jax
import jax.numpy as jnp
from jax import lax
from jax.experimental import pallas as pl
from jax.experimental.pallas import tpu as pltpu
from jax.sharding import PartitionSpec as P


F32 = jnp.float32
BF16 = jnp.bfloat16
FINISH_SPAN = 4
APPLY_SPAN = 4
TILE = 16
LANES = 128


def passed_along(x, axis, by):
    count = lax.axis_size(axis)
    pairs = [(i, i + by) for i in range(count) if 0 <= i + by < count]
    return lax.ppermute(x, axis, pairs)


def exchange(x):
    return lax.all_to_all(x, "seq", split_axis=0, concat_axis=0, tiled=True)


def dot_nt(left, right):
    return lax.dot_general(
        left, right, (((1,), (1,)), ((), ())), preferred_element_type=F32
    )


def dot_nn(left, right):
    return lax.dot_general(
        left, right, (((1,), (0,)), ((), ())), preferred_element_type=F32
    )


def grid_index(shape, dim):
    return lax.broadcasted_iota(jnp.int32, shape, dim)


def identity(size):
    shape = (size, size)
    return (grid_index(shape, 0) == grid_index(shape, 1)).astype(F32).astype(BF16)


def delayed(x, before, held):
    rows = x.shape[0]
    held[pl.ds(6, 2), :] = before
    held[pl.ds(8, rows), :] = x
    return held[pl.ds(7, rows), :], held[pl.ds(6, rows), :]


def advanced(x, after, held):
    rows = x.shape[0]
    held[pl.ds(0, rows), :] = x
    held[pl.ds(rows, 2), :] = after
    return held[pl.ds(1, rows), :], held[pl.ds(2, rows), :]


def edge_kernel(query_ref, key_ref, value_ref, key_top, value_top, grad_top, last_ref, first_ref):
    for i, ref in enumerate((query_ref, key_ref, value_ref)):
        last_ref[i] = ref[...].astype(F32)[6:8].astype(BF16)
    for i, ref in enumerate((key_top, value_top, grad_top)):
        first_ref[i] = ref[...].astype(F32)[0:2].astype(BF16)


def weighted(taps, branch, x, one, two):
    base = 3 * branch
    out = taps[base : base + 1] * x
    out = out + taps[base + 1 : base + 2] * one
    return out + taps[base + 2 : base + 3] * two


def next_featured(taps, branch, x, new):
    last = x[-8:][6:8]
    one = jnp.concatenate([last[1:2], new[0:1]], axis=0)
    return weighted(taps, branch, new, one, last)


def partner(rank, step, count, sign):
    if count & (count - 1):
        return lax.rem(rank + sign * step + count, jnp.int32(count))
    return rank ^ step


def send_kernel(
    first_chunk, chunks, spread, rank_ref, query_ref, key_ref, value_ref, grad_ref, before_ref, taps_ref, filter_ref,
    *refs,
):
    outs, held = refs[:-1], refs[-1]
    seq = query_ref.shape[1] // LANES
    all_groups = filter_ref.shape[1]
    count = all_groups // chunks
    groups = count // seq
    unit = identity(LANES)
    rounded = filter_ref[...].astype(BF16)
    row = grid_index((TILE, all_groups), 0)
    column = grid_index((TILE, all_groups), 1)
    for step in range(seq):
        d = partner(rank_ref[0], step, seq, 1) if spread else step
        out = outs[step] if spread else outs[0].at[step]
        cols = pl.ds(pl.multiple_of(d * LANES, LANES) if spread else d * LANES, LANES)
        taps = taps_ref[:, 0, cols]
        feats = []
        for branch, ref in enumerate((query_ref, key_ref, value_ref)):
            x = ref[:, cols].astype(F32)
            one, two = delayed(x, before_ref[branch, :, cols].astype(F32), held.at[step % 2, branch])
            feats.append(weighted(taps, branch, x, one, two))
        product = (feats[1] * feats[2]).astype(BF16)
        scaled = (grad_ref[:, cols].astype(F32) * feats[0]).astype(BF16)
        out[pl.ds(0, LANES), :] = dot_nt(unit, product).astype(BF16)
        out[pl.ds(LANES, LANES), :] = dot_nt(unit, scaled).astype(BF16)
        wanted = (first_chunk + pl.program_id(0)) * count + d * groups + row
        pick = ((row < groups) & (column == wanted)).astype(F32).astype(BF16)
        out[pl.ds(2 * LANES, TILE), :] = dot_nt(pick, rounded).astype(BF16)


def toeplitz_blocks(lines):
    base = [
        pltpu.roll(jnp.broadcast_to(line, (8, LANES)), 0, 1, stride=1, stride_axis=0)
        for line in lines
    ]
    lane = grid_index((8, LANES), 1)
    sub = grid_index((8, LANES), 0)
    zero = jnp.zeros((8, LANES), F32)
    parts = [[] for _ in lines]
    for m in range(LANES // 8):
        below = zero
        for k, start in enumerate(base):
            turned = pltpu.roll(start, 8 * m, 1) if m else start
            parts[k].append(jnp.where(lane >= sub + 8 * m, turned, below))
            below = turned
    return [jnp.concatenate(part, axis=0).astype(BF16) for part in parts]


def diagonal_sums(cross, blocks):
    parts = [cross[:, k * LANES : (k + 1) * LANES] for k in range(blocks)]
    rows = LANES
    while rows > 8:
        half = rows // 2
        lane = grid_index((half, LANES), 1)
        turned = [pltpu.roll(part[half:rows], LANES - half, 1) for part in parts]
        turned.append(jnp.zeros((half, LANES), F32))
        parts = [
            parts[k][:half] + jnp.where(lane < LANES - half, turned[k], turned[k + 1])
            for k in range(blocks)
        ]
        rows = half
    lane = grid_index((8, LANES), 1)
    sub = grid_index((8, LANES), 0)
    turned = [pltpu.roll(part, LANES - 7, 1, stride=1, stride_axis=0) for part in parts]
    turned.append(jnp.zeros((8, LANES), F32))
    keep = lane < sub + (LANES - 7)
    return [
        jnp.sum(jnp.where(keep, turned[k], turned[k + 1]), axis=0, keepdims=True)
        for k in range(blocks)
    ]


def conv_kernel(groups, chunk, count, scale, *refs):
    if chunk is None:
        in_ref = refs[0]
        refs = refs[1:]
    else:
        in_ref = refs[-1]
        for step in range(count):
            in_ref[partner(refs[0][0], step, count, -1)] = refs[1 + step][...]
        refs = refs[1 + count : -1]
    out_ref, corr, taps, even_taps, odd_taps, even_cross, odd_cross = refs
    blocks = in_ref.shape[0]
    wide = LANES // groups
    rows = blocks * wide
    lane = grid_index((LANES, LANES), 1)
    sub = grid_index((LANES, LANES), 0)
    flipped = (sub // 8) * 8 + 7 - sub % 8
    flip = (lane == flipped).astype(F32).astype(BF16)
    taps[...] = in_ref[:, pl.ds(2 * LANES, TILE), :].astype(F32)
    odd_cross[...] = jnp.zeros(odd_cross.shape, F32)

    def spread(g, table):
        lines = [taps[k, pl.ds(g, 1), :] for k in range(blocks)]
        for k, block in enumerate(toeplitz_blocks(lines)):
            table[:, pl.ds(k * LANES, LANES)] = block

    def multiply(g, table, cross):
        at = pl.multiple_of(g * wide, wide)
        first = in_ref[:, pl.ds(at, wide), :].reshape(rows, LANES)
        second = in_ref[:, pl.ds(LANES + at, wide), :].reshape(rows, LANES)
        shifted, ahead = [first], [second]
        for k in range(1, blocks):
            gap = jnp.zeros((wide * k, LANES), BF16)
            shifted.append(jnp.concatenate([gap, first[: rows - wide * k]], axis=0))
            ahead.append(jnp.concatenate([second[wide * k :], gap], axis=0))
        ahead = jnp.concatenate(ahead, axis=1)
        stacked = [table[:, pl.ds(k * LANES, LANES)] for k in range(blocks)]
        conv = dot_nn(jnp.concatenate(shifted, axis=1), jnp.concatenate(stacked, axis=0))
        back = dot_nt(ahead, table[...])
        out_ref[:, pl.ds(at, wide), :] = conv.astype(BF16).reshape(blocks, wide, LANES)
        out_ref[:, pl.ds(LANES + at, wide), :] = back.astype(BF16).reshape(blocks, wide, LANES)
        cross[...] = dot_nn(dot_nt(flip, first).astype(BF16), ahead)

    def collect(g, cross):
        for k, line in enumerate(diagonal_sums(cross[...], blocks)):
            corr[k, pl.ds(g, 1), :] = line * scale

    spread(0, even_taps)

    def two_groups(step, carry):
        g = 2 * step
        spread(g + 1, odd_taps)
        multiply(g, even_taps, even_cross)
        collect(jnp.maximum(g - 1, 0), odd_cross)
        spread(jnp.minimum(g + 2, groups - 1), even_taps)
        multiply(g + 1, odd_taps, odd_cross)
        collect(g, even_cross)
        return carry

    lax.fori_loop(0, groups // 2, two_groups, 0)
    collect(groups - 1, odd_cross)
    pick_row = grid_index((TILE, 2 * LANES), 0)
    pick_lane = grid_index((TILE, 2 * LANES), 1)
    wanted = (pick_row // 2) * LANES + pick_row % 2
    pick = ((pick_row < 4) & (pick_lane == wanted)).astype(F32).astype(BF16)
    for a in range(blocks):
        if a + 1 < blocks:
            both = [out_ref[a + 1, pl.ds(0, LANES), :], out_ref[a + 1, pl.ds(LANES, LANES), :]]
            line = dot_nt(pick, jnp.concatenate(both, axis=1)).astype(BF16)
        else:
            line = jnp.zeros((TILE, LANES), BF16)
        out_ref[a, pl.ds(2 * LANES, TILE), :] = line
        full = corr[a]
        high = full.astype(BF16).astype(F32)
        pair = jnp.concatenate([high, full - high], axis=0).astype(BF16)
        out_ref[a, pl.ds(2 * LANES + TILE, 2 * groups), :] = pair


def finish_kernel(
    scale, has_old, query_ref, key_ref, value_ref, grad_ref, before_ref, after_ref, taps_ref, in_ref, *refs
):
    layer_ref, late_ref, sums_ref, corr_ref, held = refs[3:] if has_old else refs
    groups = corr_ref.shape[0] // in_ref.shape[0]
    rows = query_ref.shape[0]
    unit = identity(LANES)
    for part in range(in_ref.shape[0]):
        cols = pl.ds(part * LANES, LANES)
        taps = taps_ref[:, 0, cols]
        conv = dot_nt(unit, in_ref[part, pl.ds(0, LANES), :])
        back = dot_nt(unit, in_ref[part, pl.ds(LANES, LANES), :])
        edge = in_ref[part, pl.ds(2 * LANES, TILE), :].astype(F32)
        grad = grad_ref[:, cols].astype(F32)
        lines = []

        def raw_of(branch, ref):
            x = ref[:, cols].astype(F32)
            before = before_ref[branch, :, cols].astype(F32)
            return (x,) + delayed(x, before, held.at[part % 2, branch])

        def tap_lines(value, raw):
            for shifted in raw:
                lines.append(jnp.sum(value * shifted, axis=0, keepdims=True) * scale)

        raw = raw_of(0, query_ref)
        layer_ref[:, cols] = (weighted(taps, 0, *raw) * conv).astype(BF16)
        value = grad * conv
        tap_lines(value, raw)
        follow = after_ref[2, :, cols].astype(F32) * edge[0:2]
        total = weighted(taps, 0, value, *advanced(value, follow, held.at[part % 2, 3]))
        late_ref[pl.ds(0, rows), cols] = total.astype(BF16)
        key_raw = raw_of(1, key_ref)
        value_raw = raw_of(2, value_ref)
        tap_lines(back * weighted(taps, 2, *value_raw), key_raw)
        tap_lines(back * weighted(taps, 1, *key_raw), value_raw)
        late_ref[pl.ds(rows, rows), cols] = back.astype(BF16)
        tail = jnp.concatenate([edge[2:4], jnp.zeros((6, LANES), F32)], axis=0)
        late_ref[pl.ds(2 * rows, 8), cols] = tail.astype(BF16)
        for index, line in enumerate(lines):
            sums_ref[index, :, cols] = line
        pair = in_ref[part, pl.ds(2 * LANES + TILE, 2 * groups), :].astype(F32)
        corr_ref[pl.ds(part * groups, groups), :] = pair[:groups] + pair[groups:]


def apply_kernel(has_old, key_ref, value_ref, edges_ref, taps_ref, late_ref, *refs):
    out_ref, held = refs[1:] if has_old else refs
    rows, width = key_ref.shape
    for part in range(width // LANES):
        cols = pl.ds(part * LANES, LANES)
        taps = taps_ref[:, 0, cols]
        back = late_ref[pl.ds(rows, rows), cols].astype(F32)
        edge = late_ref[pl.ds(2 * rows, 8), cols].astype(F32)[0:2]
        out_ref[0, :, cols] = late_ref[pl.ds(0, rows), cols]
        for branch, ref in ((0, value_ref), (1, key_ref)):
            other = 1 - branch
            x = ref[:, cols].astype(F32)
            one, two = delayed(x, edges_ref[other, :, cols].astype(F32), held.at[part % 2, branch])
            value = back * weighted(taps, other, x, one, two)
            new = edges_ref[2 + other, :, cols].astype(F32)
            follow = edge * next_featured(taps, other, x, new)
            one, two = advanced(value, follow, held.at[part % 2, branch + 2])
            out_ref[branch + 1, :, cols] = weighted(taps, branch, value, one, two).astype(BF16)


def summed(x, axis):
    count = lax.axis_size(axis)
    if count & (count - 1):
        return lax.psum(x, axis)
    for bit in range(count.bit_length() - 1):
        x = x + lax.ppermute(x, axis, [(i, i ^ (1 << bit)) for i in range(count)])
    return x


def batches(chunks):
    return [(0, 1), (1, chunks)] if chunks > 1 else [(0, 1)]


def layer_step(query_in, key_in, value_in, grad_out, long_filter, short_taps):
    seq = lax.axis_size("seq")
    rows, width = query_in.shape[1:]
    groups = long_filter.shape[2]
    total_rows = rows * seq
    wide = width // groups
    across = LANES * seq
    chunks = width // across
    own_groups = LANES // wide
    height = 2 * LANES + TILE
    back_height = height + 2 * own_groups
    span = math.gcd(FINISH_SPAN, seq)
    steps = seq // span
    last_span = math.gcd(APPLY_SPAN, seq)
    last_steps = seq // last_span
    query, key, value, grad = (
        pltpu.with_memory_space_constraint(x[0], pltpu.HBM) for x in (query_in, key_in, value_in, grad_out)
    )
    taps = short_taps[0].reshape(9, 1, width)
    low = pl.BlockSpec((8, width), lambda i: (rows // 8 - 1, 0))
    high = pl.BlockSpec((8, width), lambda i: (0, 0))
    two_rows = pl.BlockSpec((3, 2, width), lambda i: (0, 0, 0))
    last, top = pl.pallas_call(
        edge_kernel,
        grid=(1,),
        in_specs=[low, low, low, high, high, high],
        out_specs=[two_rows, two_rows],
        out_shape=[jax.ShapeDtypeStruct((3, 2, width), BF16)] * 2,
        name="edges",
        compiler_params=pltpu.CompilerParams(vmem_limit_bytes=32 * 2**20),
    )(query, key, value, key, value, grad)
    before = passed_along(last, "seq", 1)
    after = passed_along(top, "seq", -1)

    rank = lax.axis_index("seq").astype(jnp.int32).reshape(1)
    scalar = pl.BlockSpec(memory_space=pltpu.SMEM)
    arrived = []
    for part, (low, high) in enumerate(batches(chunks)):
        main = pl.BlockSpec((rows, across), lambda c, low=low: (0, low + c))
        if part:
            out_specs = [pl.BlockSpec((height, rows), lambda c: (c, 0))] * seq
            out_shape = [jax.ShapeDtypeStruct(((high - low) * height, rows), BF16)] * seq
        else:
            out_specs = [pl.BlockSpec((seq, height, rows), lambda c: (0, c, 0))]
            out_shape = [jax.ShapeDtypeStruct((seq, height, rows), BF16)]
        sent = pl.pallas_call(
            functools.partial(send_kernel, low, chunks, part > 0),
            grid=(high - low,),
            in_specs=[
                scalar, main, main, main, main,
                pl.BlockSpec((3, 2, across), lambda c, low=low: (0, 0, low + c)),
                pl.BlockSpec((9, 1, across), lambda c, low=low: (0, 0, low + c)),
                pl.BlockSpec((rows, groups), lambda c: (0, 0)),
            ],
            out_specs=out_specs,
            out_shape=out_shape,
            scratch_shapes=[pltpu.VMEM((2, 3, rows + 8, LANES), F32)],
            name="send",
            compiler_params=pltpu.CompilerParams(vmem_limit_bytes=32 * 2**20),
        )(rank, query, key, value, grad, before, taps, long_filter[0])
        if not part:
            arrived.append((None, (exchange(sent[0]),)))
            continue
        there = [sent[0]]
        for step in range(1, seq):
            pairs = [(i, i ^ step if seq & (seq - 1) == 0 else (i + step) % seq) for i in range(seq)]
            there.append(lax.ppermute(sent[step], "seq", pairs))
        arrived += [(chunk, (rank, *there)) for chunk in range(high - low)]

    early = {}
    edges = jnp.concatenate([before[1:], after[:2]], axis=0)
    for name, array in (("key", key), ("value", value), ("edges", edges), ("taps", taps[3:])):
        early[name] = passed_along(array, "pipe", -1)

    layer, passed, tap_sums, corr = None, None, None, None
    for chunk in range(chunks):
        place, there = arrived[chunk]
        returned = pl.pallas_call(
            functools.partial(conv_kernel, own_groups, place, seq, 1.0 / math.sqrt(total_rows * wide)),
            grid=(1,),
            in_specs=[pl.BlockSpec((seq, height, rows), lambda i: (0, 0, 0))]
            if place is None
            else [scalar] + [pl.BlockSpec((height, rows), lambda i, place=place: (place, 0))] * seq,
            out_specs=pl.BlockSpec((seq, back_height, rows), lambda i: (0, 0, 0)),
            out_shape=jax.ShapeDtypeStruct((seq, back_height, rows), BF16),
            scratch_shapes=[pltpu.VMEM((seq, own_groups, LANES), F32), pltpu.VMEM((seq, TILE, LANES), F32)]
            + [pltpu.VMEM((LANES, total_rows), BF16)] * 2
            + [pltpu.VMEM((LANES, total_rows), F32)] * 2
            + [pltpu.VMEM((seq, height, LANES), BF16)] * (place is not None),
            name="conv",
            compiler_params=pltpu.CompilerParams(vmem_limit_bytes=24 * 2**20),
        )(*there)
        back = exchange(returned)
        at = lambda i, chunk=chunk: (0, chunk * steps + i)
        at3 = lambda i, chunk=chunk: (0, 0, chunk * steps + i)
        last = lambda i, chunk=chunk: (0, chunk * last_steps + i)
        last3 = lambda i, chunk=chunk: (0, 0, chunk * last_steps + i)
        main = pl.BlockSpec((rows, span * LANES), at)
        edge = pl.BlockSpec((3, 2, span * LANES), at3)
        tap_spec = pl.BlockSpec((9, 1, span * LANES), at3)
        here = pl.BlockSpec((2 * rows + 8, span * LANES), lambda i: (0, i))
        has_old = layer is not None
        old = [pl.BlockSpec(memory_space=pl.ANY)] * has_old
        layer, late, tap_sums, corr = pl.pallas_call(
            functools.partial(finish_kernel, 1.0 / math.sqrt(total_rows), has_old),
            grid=(steps,),
            in_specs=[
                main, main, main, main, edge, edge, tap_spec,
                pl.BlockSpec((span, back_height, rows), lambda i: (i, 0, 0)),
            ]
            + old * 3,
            out_specs=[
                main, here, tap_spec,
                pl.BlockSpec((span * own_groups, rows), lambda i, chunk=chunk: (chunk * steps + i, 0)),
            ],
            out_shape=[
                jax.ShapeDtypeStruct((rows, width), BF16),
                jax.ShapeDtypeStruct((2 * rows + 8, across), BF16),
                jax.ShapeDtypeStruct((9, 1, width), F32),
                jax.ShapeDtypeStruct((groups, rows), F32),
            ],
            input_output_aliases={8: 0, 9: 2, 10: 3} if has_old else {},
            scratch_shapes=[pltpu.VMEM((2, 4, rows + 8, LANES), F32)],
            name="finish",
            compiler_params=pltpu.CompilerParams(vmem_limit_bytes=32 * 2**20),
        )(query, key, value, grad, before, after, taps, back, *([layer, tap_sums, corr] if has_old else []))
        late = passed_along(late, "pipe", -1)
        passed = pl.pallas_call(
            functools.partial(apply_kernel, has_old),
            grid=(last_steps,),
            in_specs=[
                pl.BlockSpec((rows, last_span * LANES), last),
                pl.BlockSpec((rows, last_span * LANES), last),
                pl.BlockSpec((4, 2, last_span * LANES), last3),
                pl.BlockSpec((6, 1, last_span * LANES), last3),
                pl.BlockSpec((2 * rows + 8, last_span * LANES), lambda i: (0, i)),
            ]
            + old,
            out_specs=pl.BlockSpec((3, rows, last_span * LANES), last3),
            out_shape=jax.ShapeDtypeStruct((3, rows, width), BF16),
            input_output_aliases={5: 0} if has_old else {},
            scratch_shapes=[pltpu.VMEM((2, 4, rows + 8, LANES), F32)],
            name="apply",
            compiler_params=pltpu.CompilerParams(vmem_limit_bytes=24 * 2**20),
        )(
            early["key"], early["value"], early["edges"], early["taps"], late,
            *([passed] * has_old),
        )

    filter_grad = corr.T
    tap_grads = summed(tap_sums, "seq").reshape(3, 3, width)
    return (layer[None], passed[None], filter_grad[None], tap_grads[None])


def solution(mesh):
    in_specs = (
        P("pipe", "seq", None),
        P("pipe", "seq", None),
        P("pipe", "seq", None),
        P("pipe", "seq", None),
        P("pipe", "seq", None),
        P("pipe", None, None, None),
    )
    out_specs = (
        P("pipe", "seq", None),
        P("pipe", None, "seq", None),
        P("pipe", "seq", None),
        P("pipe", None, None, None),
    )
    return jax.shard_map(layer_step, mesh=mesh, in_specs=in_specs, out_specs=out_specs, check_vma=False)
```

```python
import functools
import math

import jax
import jax.numpy as jnp
from jax import lax
from jax.experimental import pallas as pl
from jax.experimental.pallas import tpu as pltpu
from jax.sharding import PartitionSpec as P


F32 = jnp.float32
BF16 = jnp.bfloat16
FINISH_SPAN = 4
APPLY_SPAN = 4
TILE = 16
LANES = 128


def passed_along(x, axis, by):
    count = lax.axis_size(axis)
    pairs = [(i, i + by) for i in range(count) if 0 <= i + by < count]
    return lax.ppermute(x, axis, pairs)


def exchange(x):
    return lax.all_to_all(x, "seq", split_axis=0, concat_axis=0, tiled=True)


def dot_nt(left, right):
    return lax.dot_general(
        left, right, (((1,), (1,)), ((), ())), preferred_element_type=F32
    )


def dot_nn(left, right):
    return lax.dot_general(
        left, right, (((1,), (0,)), ((), ())), preferred_element_type=F32
    )


def grid_index(shape, dim):
    return lax.broadcasted_iota(jnp.int32, shape, dim)


def identity(size):
    shape = (size, size)
    return (grid_index(shape, 0) == grid_index(shape, 1)).astype(F32).astype(BF16)


def delayed(x, before, held):
    rows = x.shape[0]
    held[pl.ds(6, 2), :] = before
    held[pl.ds(8, rows), :] = x
    return held[pl.ds(7, rows), :], held[pl.ds(6, rows), :]


def advanced(x, after, held):
    rows = x.shape[0]
    held[pl.ds(0, rows), :] = x
    held[pl.ds(rows, 2), :] = after
    return held[pl.ds(1, rows), :], held[pl.ds(2, rows), :]


def edge_kernel(query_ref, key_ref, value_ref, key_top, value_top, grad_top, last_ref, first_ref):
    for i, ref in enumerate((query_ref, key_ref, value_ref)):
        last_ref[i] = ref[...].astype(F32)[6:8].astype(BF16)
    for i, ref in enumerate((key_top, value_top, grad_top)):
        first_ref[i] = ref[...].astype(F32)[0:2].astype(BF16)


def weighted(taps, branch, x, one, two):
    base = 3 * branch
    out = taps[base : base + 1] * x
    out = out + taps[base + 1 : base + 2] * one
    return out + taps[base + 2 : base + 3] * two


def next_featured(taps, branch, x, new):
    last = x[-8:][6:8]
    one = jnp.concatenate([last[1:2], new[0:1]], axis=0)
    return weighted(taps, branch, new, one, last)


def partner(rank, step, count, sign):
    if count & (count - 1):
        return lax.rem(rank + sign * step + count, jnp.int32(count))
    return rank ^ step


def send_kernel(
    first_chunk, chunks, spread, rank_ref, query_ref, key_ref, value_ref, grad_ref, before_ref, taps_ref, filter_ref,
    *refs,
):
    outs, held = refs[:-1], refs[-1]
    seq = query_ref.shape[1] // LANES
    all_groups = filter_ref.shape[1]
    count = all_groups // chunks
    groups = count // seq
    unit = identity(LANES)
    rounded = filter_ref[...].astype(BF16)
    row = grid_index((TILE, all_groups), 0)
    column = grid_index((TILE, all_groups), 1)
    for step in range(seq):
        d = partner(rank_ref[0], step, seq, 1) if spread else step
        out = outs[step] if spread else outs[0].at[step]
        cols = pl.ds(pl.multiple_of(d * LANES, LANES) if spread else d * LANES, LANES)
        taps = taps_ref[:, 0, cols]
        feats = []
        for branch, ref in enumerate((query_ref, key_ref, value_ref)):
            x = ref[:, cols].astype(F32)
            one, two = delayed(x, before_ref[branch, :, cols].astype(F32), held.at[step % 2, branch])
            feats.append(weighted(taps, branch, x, one, two))
        product = (feats[1] * feats[2]).astype(BF16)
        scaled = (grad_ref[:, cols].astype(F32) * feats[0]).astype(BF16)
        out[pl.ds(0, LANES), :] = dot_nt(unit, product).astype(BF16)
        out[pl.ds(LANES, LANES), :] = dot_nt(unit, scaled).astype(BF16)
        wanted = (first_chunk + pl.program_id(0)) * count + d * groups + row
        pick = ((row < groups) & (column == wanted)).astype(F32).astype(BF16)
        out[pl.ds(2 * LANES, TILE), :] = dot_nt(pick, rounded).astype(BF16)


def toeplitz_blocks(lines):
    base = [
        pltpu.roll(jnp.broadcast_to(line, (8, LANES)), 0, 1, stride=1, stride_axis=0)
        for line in lines
    ]
    lane = grid_index((8, LANES), 1)
    sub = grid_index((8, LANES), 0)
    zero = jnp.zeros((8, LANES), F32)
    parts = [[] for _ in lines]
    for m in range(LANES // 8):
        below = zero
        for k, start in enumerate(base):
            turned = pltpu.roll(start, 8 * m, 1) if m else start
            parts[k].append(jnp.where(lane >= sub + 8 * m, turned, below))
            below = turned
    return [jnp.concatenate(part, axis=0).astype(BF16) for part in parts]


def diagonal_sums(cross, blocks):
    parts = [cross[:, k * LANES : (k + 1) * LANES] for k in range(blocks)]
    rows = LANES
    while rows > 8:
        half = rows // 2
        lane = grid_index((half, LANES), 1)
        turned = [pltpu.roll(part[half:rows], LANES - half, 1) for part in parts]
        turned.append(jnp.zeros((half, LANES), F32))
        parts = [
            parts[k][:half] + jnp.where(lane < LANES - half, turned[k], turned[k + 1])
            for k in range(blocks)
        ]
        rows = half
    lane = grid_index((8, LANES), 1)
    sub = grid_index((8, LANES), 0)
    turned = [pltpu.roll(part, LANES - 7, 1, stride=1, stride_axis=0) for part in parts]
    turned.append(jnp.zeros((8, LANES), F32))
    keep = lane < sub + (LANES - 7)
    return [
        jnp.sum(jnp.where(keep, turned[k], turned[k + 1]), axis=0, keepdims=True)
        for k in range(blocks)
    ]


def conv_kernel(groups, spread_out, chunk, count, height, scale, *refs):
    if not spread_out:
        in_ref = refs[0].at[:, pl.ds(chunk * height, height), :]
        refs = refs[1:]
    else:
        in_ref = refs[-1]
        for step in range(count):
            block = refs[1 + step][pl.ds(chunk * height, height), :]
            in_ref[partner(refs[0][0], step, count, -1)] = block
        refs = refs[1 + count : -1]
    out_ref, corr, taps, even_taps, odd_taps, even_cross, odd_cross = refs
    blocks = in_ref.shape[0]
    wide = LANES // groups
    rows = blocks * wide
    lane = grid_index((LANES, LANES), 1)
    sub = grid_index((LANES, LANES), 0)
    flipped = (sub // 8) * 8 + 7 - sub % 8
    flip = (lane == flipped).astype(F32).astype(BF16)
    taps[...] = in_ref[:, pl.ds(2 * LANES, TILE), :].astype(F32)
    odd_cross[...] = jnp.zeros(odd_cross.shape, F32)

    def spread(g, table):
        lines = [taps[k, pl.ds(g, 1), :] for k in range(blocks)]
        for k, block in enumerate(toeplitz_blocks(lines)):
            table[:, pl.ds(k * LANES, LANES)] = block

    def multiply(g, table, cross):
        at = pl.multiple_of(g * wide, wide)
        first = in_ref[:, pl.ds(at, wide), :].reshape(rows, LANES)
        second = in_ref[:, pl.ds(LANES + at, wide), :].reshape(rows, LANES)
        shifted, ahead = [first], [second]
        for k in range(1, blocks):
            gap = jnp.zeros((wide * k, LANES), BF16)
            shifted.append(jnp.concatenate([gap, first[: rows - wide * k]], axis=0))
            ahead.append(jnp.concatenate([second[wide * k :], gap], axis=0))
        ahead = jnp.concatenate(ahead, axis=1)
        stacked = [table[:, pl.ds(k * LANES, LANES)] for k in range(blocks)]
        conv = dot_nn(jnp.concatenate(shifted, axis=1), jnp.concatenate(stacked, axis=0))
        back = dot_nt(ahead, table[...])
        out_ref[:, pl.ds(at, wide), :] = conv.astype(BF16).reshape(blocks, wide, LANES)
        out_ref[:, pl.ds(LANES + at, wide), :] = back.astype(BF16).reshape(blocks, wide, LANES)
        cross[...] = dot_nn(dot_nt(flip, first).astype(BF16), ahead)

    def collect(g, cross):
        for k, line in enumerate(diagonal_sums(cross[...], blocks)):
            corr[k, pl.ds(g, 1), :] = line * scale

    spread(0, even_taps)

    def two_groups(step, carry):
        g = 2 * step
        spread(g + 1, odd_taps)
        multiply(g, even_taps, even_cross)
        collect(jnp.maximum(g - 1, 0), odd_cross)
        spread(jnp.minimum(g + 2, groups - 1), even_taps)
        multiply(g + 1, odd_taps, odd_cross)
        collect(g, even_cross)
        return carry

    lax.fori_loop(0, groups // 2, two_groups, 0)
    collect(groups - 1, odd_cross)
    pick_row = grid_index((TILE, 2 * LANES), 0)
    pick_lane = grid_index((TILE, 2 * LANES), 1)
    wanted = (pick_row // 2) * LANES + pick_row % 2
    pick = ((pick_row < 4) & (pick_lane == wanted)).astype(F32).astype(BF16)
    for a in range(blocks):
        if a + 1 < blocks:
            both = [out_ref[a + 1, pl.ds(0, LANES), :], out_ref[a + 1, pl.ds(LANES, LANES), :]]
            line = dot_nt(pick, jnp.concatenate(both, axis=1)).astype(BF16)
        else:
            line = jnp.zeros((TILE, LANES), BF16)
        out_ref[a, pl.ds(2 * LANES, TILE), :] = line
        full = corr[a]
        high = full.astype(BF16).astype(F32)
        pair = jnp.concatenate([high, full - high], axis=0).astype(BF16)
        out_ref[a, pl.ds(2 * LANES + TILE, 2 * groups), :] = pair


def finish_kernel(
    scale, has_old, query_ref, key_ref, value_ref, grad_ref, before_ref, after_ref, taps_ref, in_ref, *refs
):
    layer_ref, late_ref, sums_ref, corr_ref, held = refs[3:] if has_old else refs
    groups = corr_ref.shape[0] // in_ref.shape[0]
    rows = query_ref.shape[0]
    unit = identity(LANES)
    for part in range(in_ref.shape[0]):
        cols = pl.ds(part * LANES, LANES)
        taps = taps_ref[:, 0, cols]
        conv = dot_nt(unit, in_ref[part, pl.ds(0, LANES), :])
        back = dot_nt(unit, in_ref[part, pl.ds(LANES, LANES), :])
        edge = in_ref[part, pl.ds(2 * LANES, TILE), :].astype(F32)
        grad = grad_ref[:, cols].astype(F32)
        lines = []

        def raw_of(branch, ref):
            x = ref[:, cols].astype(F32)
            before = before_ref[branch, :, cols].astype(F32)
            return (x,) + delayed(x, before, held.at[part % 2, branch])

        def tap_lines(value, raw):
            for shifted in raw:
                lines.append(jnp.sum(value * shifted, axis=0, keepdims=True) * scale)

        raw = raw_of(0, query_ref)
        layer_ref[:, cols] = (weighted(taps, 0, *raw) * conv).astype(BF16)
        value = grad * conv
        tap_lines(value, raw)
        follow = after_ref[2, :, cols].astype(F32) * edge[0:2]
        total = weighted(taps, 0, value, *advanced(value, follow, held.at[part % 2, 3]))
        late_ref[pl.ds(0, rows), cols] = total.astype(BF16)
        key_raw = raw_of(1, key_ref)
        value_raw = raw_of(2, value_ref)
        tap_lines(back * weighted(taps, 2, *value_raw), key_raw)
        tap_lines(back * weighted(taps, 1, *key_raw), value_raw)
        late_ref[pl.ds(rows, rows), cols] = back.astype(BF16)
        tail = jnp.concatenate([edge[2:4], jnp.zeros((6, LANES), F32)], axis=0)
        late_ref[pl.ds(2 * rows, 8), cols] = tail.astype(BF16)
        for index, line in enumerate(lines):
            sums_ref[index, :, cols] = line
        pair = in_ref[part, pl.ds(2 * LANES + TILE, 2 * groups), :].astype(F32)
        corr_ref[pl.ds(part * groups, groups), :] = pair[:groups] + pair[groups:]


def apply_kernel(has_old, key_ref, value_ref, edges_ref, taps_ref, late_ref, *refs):
    out_ref, held = refs[1:] if has_old else refs
    rows, width = key_ref.shape
    for part in range(width // LANES):
        cols = pl.ds(part * LANES, LANES)
        taps = taps_ref[:, 0, cols]
        back = late_ref[pl.ds(rows, rows), cols].astype(F32)
        edge = late_ref[pl.ds(2 * rows, 8), cols].astype(F32)[0:2]
        out_ref[0, :, cols] = late_ref[pl.ds(0, rows), cols]
        for branch, ref in ((0, value_ref), (1, key_ref)):
            other = 1 - branch
            x = ref[:, cols].astype(F32)
            one, two = delayed(x, edges_ref[other, :, cols].astype(F32), held.at[part % 2, branch])
            value = back * weighted(taps, other, x, one, two)
            new = edges_ref[2 + other, :, cols].astype(F32)
            follow = edge * next_featured(taps, other, x, new)
            one, two = advanced(value, follow, held.at[part % 2, branch + 2])
            out_ref[branch + 1, :, cols] = weighted(taps, branch, value, one, two).astype(BF16)


def summed(x, axis):
    count = lax.axis_size(axis)
    if count & (count - 1):
        return lax.psum(x, axis)
    for bit in range(count.bit_length() - 1):
        x = x + lax.ppermute(x, axis, [(i, i ^ (1 << bit)) for i in range(count)])
    return x


def batches(chunks):
    first = (chunks + 1) // 2
    return [(0, first), (first, chunks)] if chunks > 1 else [(0, 1)]


def layer_step(query_in, key_in, value_in, grad_out, long_filter, short_taps):
    seq = lax.axis_size("seq")
    rows, width = query_in.shape[1:]
    groups = long_filter.shape[2]
    total_rows = rows * seq
    wide = width // groups
    across = LANES * seq
    chunks = width // across
    own_groups = LANES // wide
    height = 2 * LANES + TILE
    back_height = height + 2 * own_groups
    span = math.gcd(FINISH_SPAN, seq)
    steps = seq // span
    last_span = math.gcd(APPLY_SPAN, seq)
    last_steps = seq // last_span
    query, key, value, grad = (
        pltpu.with_memory_space_constraint(x[0], pltpu.HBM) for x in (query_in, key_in, value_in, grad_out)
    )
    taps = short_taps[0].reshape(9, 1, width)
    low = pl.BlockSpec((8, width), lambda i: (rows // 8 - 1, 0))
    high = pl.BlockSpec((8, width), lambda i: (0, 0))
    two_rows = pl.BlockSpec((3, 2, width), lambda i: (0, 0, 0))
    last, top = pl.pallas_call(
        edge_kernel,
        grid=(1,),
        in_specs=[low, low, low, high, high, high],
        out_specs=[two_rows, two_rows],
        out_shape=[jax.ShapeDtypeStruct((3, 2, width), BF16)] * 2,
        name="edges",
        compiler_params=pltpu.CompilerParams(vmem_limit_bytes=32 * 2**20),
    )(query, key, value, key, value, grad)
    before = passed_along(last, "seq", 1)
    after = passed_along(top, "seq", -1)

    rank = lax.axis_index("seq").astype(jnp.int32).reshape(1)
    scalar = pl.BlockSpec(memory_space=pltpu.SMEM)
    whole = pl.BlockSpec(memory_space=pltpu.VMEM)
    arrived = []
    for part, (low, high) in enumerate(batches(chunks)):
        main = pl.BlockSpec((rows, across), lambda c, low=low: (0, low + c))
        if part:
            out_specs = [pl.BlockSpec((height, rows), lambda c: (c, 0))] * seq
            out_shape = [jax.ShapeDtypeStruct(((high - low) * height, rows), BF16)] * seq
        else:
            out_specs = [pl.BlockSpec((seq, height, rows), lambda c: (0, c, 0))]
            out_shape = [jax.ShapeDtypeStruct((seq, (high - low) * height, rows), BF16)]
        sent = pl.pallas_call(
            functools.partial(send_kernel, low, chunks, part > 0),
            grid=(high - low,),
            in_specs=[
                scalar, main, main, main, main,
                pl.BlockSpec((3, 2, across), lambda c, low=low: (0, 0, low + c)),
                pl.BlockSpec((9, 1, across), lambda c, low=low: (0, 0, low + c)),
                pl.BlockSpec((rows, groups), lambda c: (0, 0)),
            ],
            out_specs=out_specs,
            out_shape=out_shape,
            scratch_shapes=[pltpu.VMEM((2, 3, rows + 8, LANES), F32)],
            name="send",
            compiler_params=pltpu.CompilerParams(vmem_limit_bytes=32 * 2**20),
        )(rank, query, key, value, grad, before, taps, long_filter[0])
        if not part:
            there = (exchange(sent[0]),)
            arrived += [(False, chunk, there) for chunk in range(high - low)]
            continue
        there = [sent[0]]
        for step in range(1, seq):
            pairs = [(i, i ^ step if seq & (seq - 1) == 0 else (i + step) % seq) for i in range(seq)]
            there.append(lax.ppermute(sent[step], "seq", pairs))
        arrived += [(True, chunk, (rank, *there)) for chunk in range(high - low)]

    early = {}
    edges = jnp.concatenate([before[1:], after[:2]], axis=0)
    for name, array in (("key", key), ("value", value), ("edges", edges), ("taps", taps[3:])):
        early[name] = passed_along(array, "pipe", -1)

    layer, passed, tap_sums, corr = None, None, None, None
    for chunk in range(chunks):
        split, place, there = arrived[chunk]
        returned = pl.pallas_call(
            functools.partial(conv_kernel, own_groups, split, place, seq, height, 1.0 / math.sqrt(total_rows * wide)),
            in_specs=[scalar] + [whole] * seq if split else [whole],
            out_specs=whole,
            out_shape=jax.ShapeDtypeStruct((seq, back_height, rows), BF16),
            scratch_shapes=[pltpu.VMEM((seq, own_groups, LANES), F32), pltpu.VMEM((seq, TILE, LANES), F32)]
            + [pltpu.VMEM((LANES, total_rows), BF16)] * 2
            + [pltpu.VMEM((LANES, total_rows), F32)] * 2
            + [pltpu.VMEM((seq, height, LANES), BF16)] * split,
            name="conv",
            compiler_params=pltpu.CompilerParams(vmem_limit_bytes=24 * 2**20),
        )(*there)
        back = exchange(returned)
        at = lambda i, chunk=chunk: (0, chunk * steps + i)
        at3 = lambda i, chunk=chunk: (0, 0, chunk * steps + i)
        last = lambda i, chunk=chunk: (0, chunk * last_steps + i)
        last3 = lambda i, chunk=chunk: (0, 0, chunk * last_steps + i)
        main = pl.BlockSpec((rows, span * LANES), at)
        edge = pl.BlockSpec((3, 2, span * LANES), at3)
        tap_spec = pl.BlockSpec((9, 1, span * LANES), at3)
        here = pl.BlockSpec((2 * rows + 8, span * LANES), lambda i: (0, i))
        has_old = layer is not None
        old = [pl.BlockSpec(memory_space=pl.ANY)] * has_old
        layer, late, tap_sums, corr = pl.pallas_call(
            functools.partial(finish_kernel, 1.0 / math.sqrt(total_rows), has_old),
            grid=(steps,),
            in_specs=[
                main, main, main, main, edge, edge, tap_spec,
                pl.BlockSpec((span, back_height, rows), lambda i: (i, 0, 0)),
            ]
            + old * 3,
            out_specs=[
                main, here, tap_spec,
                pl.BlockSpec((span * own_groups, rows), lambda i, chunk=chunk: (chunk * steps + i, 0)),
            ],
            out_shape=[
                jax.ShapeDtypeStruct((rows, width), BF16),
                jax.ShapeDtypeStruct((2 * rows + 8, across), BF16),
                jax.ShapeDtypeStruct((9, 1, width), F32),
                jax.ShapeDtypeStruct((groups, rows), F32),
            ],
            input_output_aliases={8: 0, 9: 2, 10: 3} if has_old else {},
            scratch_shapes=[pltpu.VMEM((2, 4, rows + 8, LANES), F32)],
            name="finish",
            compiler_params=pltpu.CompilerParams(vmem_limit_bytes=32 * 2**20),
        )(query, key, value, grad, before, after, taps, back, *([layer, tap_sums, corr] if has_old else []))
        late = passed_along(late, "pipe", -1)
        passed = pl.pallas_call(
            functools.partial(apply_kernel, has_old),
            grid=(last_steps,),
            in_specs=[
                pl.BlockSpec((rows, last_span * LANES), last),
                pl.BlockSpec((rows, last_span * LANES), last),
                pl.BlockSpec((4, 2, last_span * LANES), last3),
                pl.BlockSpec((6, 1, last_span * LANES), last3),
                pl.BlockSpec((2 * rows + 8, last_span * LANES), lambda i: (0, i)),
            ]
            + old,
            out_specs=pl.BlockSpec((3, rows, last_span * LANES), last3),
            out_shape=jax.ShapeDtypeStruct((3, rows, width), BF16),
            input_output_aliases={5: 0} if has_old else {},
            scratch_shapes=[pltpu.VMEM((2, 4, rows + 8, LANES), F32)],
            name="apply",
            compiler_params=pltpu.CompilerParams(vmem_limit_bytes=24 * 2**20),
        )(
            early["key"], early["value"], early["edges"], early["taps"], late,
            *([passed] * has_old),
        )

    filter_grad = corr.T
    tap_grads = summed(tap_sums, "seq").reshape(3, 3, width)
    return (layer[None], passed[None], filter_grad[None], tap_grads[None])


def solution(mesh):
    in_specs = (
        P("pipe", "seq", None),
        P("pipe", "seq", None),
        P("pipe", "seq", None),
        P("pipe", "seq", None),
        P("pipe", "seq", None),
        P("pipe", None, None, None),
    )
    out_specs = (
        P("pipe", "seq", None),
        P("pipe", None, "seq", None),
        P("pipe", "seq", None),
        P("pipe", None, None, None),
    )
    return jax.shard_map(layer_step, mesh=mesh, in_specs=in_specs, out_specs=out_specs, check_vma=False)
```
